256 devices in a mesh: struct: 16 (over z, x_hi), atom: 16 (over x_lo, y, core).
Axes of the slice: x: 4 (x_hi: 2, x_lo: 2; x = x_hi * 2 + x_lo), y: 4, z: 8, core: 2. Of those that a mesh axis runs over, the one named last changes fastest.
Arguments:
- atoms_in: bfloat16 [64, 6144, 128], P('struct', 'atom'), parts along dimension 0, may hold values from -6 to 6
- cond: bfloat16 [98304, 128], P(('struct', 'atom')), parts along dimension 0, may hold values from -6 to 6
- pair: bfloat16 [3072, 32, 16, 128], P(('struct', 'atom')), parts along dimension 0, may hold values from -6 to 6
- atom_mask: int32 [98304], P(('struct', 'atom')), parts along dimension 0, may hold values 0 or 1
- atom_count: int32 [16], P('struct'), parts along dimension 0, may hold values from 5952 to 6144
- atom_to_token: int32 [98304], P(('struct', 'atom')), parts along dimension 0, may hold values from 0 to 767, as said below
- ada_weight: bfloat16 [2, 128, 256], replicated, may hold values from -0.5 to 0.5
- ada_bias: float32 [2, 128], replicated, may hold values from -1.5 to 1.5
- zero_weight: bfloat16 [2, 128, 128], replicated, may hold values from -0.5 to 0.5
- zero_bias: float32 [2, 128], replicated, may hold values from -2 to 2
- qkvg_weight: bfloat16 [128, 512], replicated, may hold values from -0.5 to 0.5
- query_bias: float32 [128], replicated, may hold values from -4 to 4
- pair_weight: float32 [4, 16], replicated, may hold values from -60 to 60
- out_weight: bfloat16 [128, 128], replicated, may hold values from -0.5 to 0.5
- swiglu_weight: bfloat16 [128, 512], replicated, may hold values from -0.5 to 0.5
- down_weight: bfloat16 [256, 128], replicated, may hold values from -0.375 to 0.375
- token_weight: bfloat16 [128, 768], replicated, may hold values from -0.5 to 0.5
Outputs:
- atoms_out: bfloat16 [64, 6144, 128], P('struct', 'atom'), parts along dimension 0
- tokens_out: bfloat16 [64, 768, 768], P('struct', 'atom'), parts along dimension 0
The draws below stay inside these ranges and needn't reach their ends.
There are 16 independent parts, one for each index of `struct`. The reference program is written for one: setup_inputs(seed, part) draws one part's arguments, and reference() takes and returns one part's arrays. A program takes and returns all parts, laid end to end along the dimension named above; an argument that names none is the same for every part. Nothing has to cross between parts.
Inputs may be any that keep to these rules, and one draw needn't show every extreme that they name: `atom_to_token`: never falls, rises by at most 1 from atom to atom, starts at 0 and ends at 767; an atom a of token t satisfies 8 * t - 8 < a < 8 * t + 2 * 8 - 1.
All inputs are finite; a program needn't handle non-finite values. No bound on the sum of `atom_mask` on one device may be relied on, other than what follows from the above.
Results may differ from the reference program's by a relative error of at most 0.01.
Values may be sent and summed in bfloat16 or wider, within the bound.
No kernel may reach another device: no remote copies, remote signals or barrier semaphores. Data moves between devices by JAX's collectives and lax.ppermute only.
A program may use at most 64 MiB of HBM per device.

```python
import jax
import jax.numpy as jnp
from jax import lax

C = 128
HEADS = 4
CP = 16
FF = 256
CT = 768
WQ = 32
WK = 128
ATOMS_PER_TOKEN = 8
SAMPLES = 4
ATOM_DEV = 384
ATOMS = 6144
TOKENS = 768
WINDOWS = 192


def draw_atom_to_token(key, part):
    pairs = (TOKENS - 2) // 2
    size = jax.random.randint(jax.random.fold_in(key, 11), (pairs,), 1, ATOMS_PER_TOKEN)
    sign = 2 * jax.random.randint(jax.random.fold_in(key, 13), (pairs,), 0, 2) - 1
    jitter = size * sign
    middle = jnp.stack([ATOMS_PER_TOKEN + jitter, ATOMS_PER_TOKEN - jitter], axis=1).reshape(-1).astype(jnp.int32)
    edge_len = jnp.full((1,), ATOMS_PER_TOKEN, jnp.int32)
    lengths = jnp.concatenate([edge_len, middle, edge_len])
    return jnp.repeat(jnp.arange(TOKENS, dtype=jnp.int32), lengths, total_repeat_length=ATOMS)


def draw_pair_weight(key, part):
    values = jax.random.normal(jax.random.fold_in(key, 23), (HEADS, CP), jnp.float32)
    return jnp.clip(values * 0.5, -2.5, 2.5)


def place_ends(drawn, own_key, low, top_value):
    place = [jax.random.randint(jax.random.fold_in(own_key, axis), (), 0, length) for axis, length in enumerate(drawn.shape)]
    main_axis = drawn.shape.index(max(drawn.shape))
    beside = place[:main_axis] + [(place[main_axis] + 1) % drawn.shape[main_axis]] + place[main_axis + 1:]
    return drawn.at[tuple(place)].set(low).at[tuple(beside)].set(top_value)


def block_scale(rng, dims, split, least, top_value):
    loudness, own = 1.0, jax.random.fold_in(rng, 6)
    for axis_at, shards_of in split:
        heights = jnp.exp(jax.random.uniform(jax.random.fold_in(own, axis_at), (shards_of,), jnp.float32, least / len(split), top_value / len(split)))
        loudness = loudness * jnp.repeat(heights, dims[axis_at] // shards_of).reshape([-1 if axis == axis_at else 1 for axis in range(len(dims))])
    return loudness


def bell_draw(own_key, shape, scale, limit, shards=(), kind=jnp.bfloat16):
    entries = scale * jax.random.normal(own_key, shape, jnp.float32)
    if shards:
        entries = entries * block_scale(own_key, shape, shards, -0.22, 0.18)
    return jnp.clip(entries, -limit, limit).astype(kind)


def setup_inputs(seed: int = 0, part: int = 0) -> dict:
    key_list = jax.random.split(jax.random.key(seed), 18)
    own_keys = jax.random.split(jax.random.fold_in(key_list[17], part), 18)
    return {
        "atoms_in": bell_draw(own_keys[0], (SAMPLES, ATOMS, C), 1.0, 6.0, ((1, 16),)),
        "cond": bell_draw(own_keys[1], (ATOMS, C), 1.0, 6.0, ((0, 16),)),
        "pair": bell_draw(own_keys[2], (WINDOWS, WQ, CP, WK), 1.0, 6.0, ((0, 16),)),
        "atom_mask": place_ends((jax.random.randint(own_keys[3], (ATOMS,), 0, 16) < 15).astype(jnp.int32), jax.random.fold_in(own_keys[3], 1), 0, 1),
        "atom_count": jax.random.randint(own_keys[4], (1,), ATOMS - ATOM_DEV // 2, ATOMS + 1).astype(jnp.int32),
        "atom_to_token": draw_atom_to_token(jax.random.fold_in(jax.random.fold_in(key_list[17], part), 71), part),
        "ada_weight": bell_draw(key_list[6], (2, C, 2 * C), C ** -0.5, 0.5),
        "ada_bias": jnp.clip(jax.random.uniform(key_list[7], (2, C), jnp.float32, -1.5, 1.5), -1.5, 1.5),
        "zero_weight": bell_draw(key_list[8], (2, C, C), C ** -0.5, 0.5),
        "zero_bias": jnp.clip(jax.random.uniform(key_list[9], (2, C), jnp.float32, -2.0, 2.0), -2.0, 2.0),
        "qkvg_weight": bell_draw(key_list[10], (C, 4 * C), C ** -0.5, 0.5),
        "query_bias": bell_draw(key_list[11], (C,), 0.7, 4.0, (), jnp.float32),
        "pair_weight": draw_pair_weight(jax.random.fold_in(key_list[17], 71), part),
        "out_weight": bell_draw(key_list[13], (C, C), C ** -0.5, 0.5),
        "swiglu_weight": bell_draw(key_list[14], (C, 2 * FF), C ** -0.5, 0.5),
        "down_weight": bell_draw(key_list[15], (FF, C), FF ** -0.5, 0.375),
        "token_weight": bell_draw(key_list[16], (C, CT), C ** -0.5, 0.5),
    }


EPS = 1e-05

def layer_norm(values, along=-1):
    center = lax.optimization_barrier(jnp.mean(values, along, keepdims=True))
    spread = lax.optimization_barrier(jnp.mean(jnp.square(values - center), along, keepdims=True))
    return (values - center) * lax.rsqrt(spread + EPS)

def window_view(extended):
    reach = WK // WQ
    blocks = extended.reshape((WINDOWS + reach - 1, WQ) + extended.shape[1:])
    return jnp.concatenate([blocks[offset:offset + WINDOWS] for offset in range(reach)], axis=1)

def reference(atoms_in, cond, pair, atom_mask, atom_count, atom_to_token, ada_weight, ada_bias, zero_weight, zero_bias, qkvg_weight, query_bias, pair_weight, out_weight, swiglu_weight, down_weight, token_weight):
    head_dim = C // HEADS
    margin = (WK - WQ) // 2
    positions = jnp.arange(ATOMS, dtype=jnp.int32)
    usable = (atom_mask == 1) & (positions < atom_count[0])
    cond_norm = layer_norm(cond.astype(jnp.float32)).astype(jnp.bfloat16)
    adapt = [jnp.dot(cond_norm, ada_weight[which], preferred_element_type=jnp.float32) for which in range(2)]
    gating = [jax.nn.sigmoid(jnp.dot(cond_norm, zero_weight[which], preferred_element_type=jnp.float32) + zero_bias[which]) for which in range(2)]

    def adaptive(stream, which):
        return layer_norm(stream) * jax.nn.sigmoid(adapt[which][:, :C] + ada_bias[which]) + adapt[which][:, C:]
    key_live = window_view(jnp.pad(usable, (margin, margin)))
    pair_norm = layer_norm(pair.astype(jnp.float32), 2)
    pair_bias = jnp.einsum('wicj,hc->whij', pair_norm, pair_weight, precision=lax.Precision.HIGHEST)
    factor = head_dim ** (-0.5)

    def one_sample(stream):
        attn_in = adaptive(stream.astype(jnp.float32), 0).astype(jnp.bfloat16)
        projected = jnp.dot(attn_in, qkvg_weight, preferred_element_type=jnp.float32)
        queries = ((projected[:, :C] + query_bias) * factor).astype(jnp.bfloat16)
        keyval = projected[:, C:3 * C].astype(jnp.bfloat16)
        gate_attn = jax.nn.sigmoid(projected[:, 3 * C:])
        windowed = window_view(jnp.pad(keyval, ((margin, margin), (0, 0))))
        query_win = queries.reshape(WINDOWS, WQ, HEADS, head_dim).astype(jnp.float32)
        keys_win = windowed[..., :C].reshape(WINDOWS, WK, HEADS, head_dim).astype(jnp.float32)
        values_win = windowed[..., C:].reshape(WINDOWS, WK, HEADS, head_dim).astype(jnp.float32)
        scores = jnp.einsum('wihd,wjhd->whij', query_win, keys_win) + pair_bias
        scores = jnp.where(key_live[:, None, None, :], scores, -1000000000.0)
        attention = jax.nn.softmax(scores, axis=-1).astype(jnp.bfloat16)
        weighted = jnp.einsum('whij,wjhd->wihd', attention.astype(jnp.float32), values_win).reshape(ATOMS, C)
        blended = (weighted * gate_attn).astype(jnp.bfloat16)
        after_attn = (stream.astype(jnp.float32) + gating[0] * jnp.dot(blended, out_weight, preferred_element_type=jnp.float32)).astype(jnp.bfloat16)
        trans_in = adaptive(after_attn.astype(jnp.float32), 1).astype(jnp.bfloat16)
        mixed = jnp.dot(trans_in, swiglu_weight, preferred_element_type=jnp.float32)
        hidden = (jax.nn.silu(mixed[:, :FF]) * mixed[:, FF:]).astype(jnp.bfloat16)
        result = (after_attn.astype(jnp.float32) + gating[1] * jnp.dot(hidden, down_weight, preferred_element_type=jnp.float32)).astype(jnp.bfloat16)
        features = jax.nn.relu(jnp.dot(result, token_weight, preferred_element_type=jnp.float32)).astype(jnp.bfloat16)
        masked = jnp.where(usable[:, None], features.astype(jnp.float32), jnp.zeros((), jnp.float32))
        totals = jax.ops.segment_sum(masked, atom_to_token, num_segments=TOKENS)
        return (result, totals)
    atoms_out, totals = lax.map(one_sample, atoms_in)
    counts = jax.ops.segment_sum(usable.astype(jnp.float32), atom_to_token, num_segments=TOKENS)
    tokens_out = (totals / jnp.maximum(counts, 1.0)[None, :, None]).astype(jnp.bfloat16)
    return (atoms_out, tokens_out)
```

```python
import functools

import jax
import jax.numpy as jnp
from jax import lax
from jax.experimental import pallas as pl
from jax.experimental.pallas import tpu as pltpu
from jax.sharding import PartitionSpec as P

ATOMS_PER_TOKEN = 8
EPS = 1e-05
HALO = 80
EDGE = 16
EDGE_Q = 8
MASKED = -1e30
BF16 = jnp.bfloat16
F32 = jnp.float32


def dot(a, b):
    return jnp.dot(a, b, preferred_element_type=F32)


def dot_t(a, b):
    return lax.dot_general(a, b, (((1,), (1,)), ((), ())), preferred_element_type=F32)


def norm_rows(x):
    center = jnp.mean(x, -1, keepdims=True)
    off = x - center
    spread = jnp.mean(jnp.square(off), -1, keepdims=True)
    return off * lax.rsqrt(spread + EPS)


def sigmoid(x):
    return 1.0 / (1.0 + jnp.exp(-x))


def iota(shape, dim):
    return lax.broadcasted_iota(jnp.int32, shape, dim)


def pack_kernel(
    count_ref, mask_ref, token_ref, atoms_ref, cond_ref, pair_ref, up_ref, down_ref, info_ref, sems
):
    samples, atom_dev, _ = atoms_ref.shape
    channels = pair_ref.shape[2]
    windows, query_len = pair_ref.shape[:2]
    copies = []

    def copy(src, dst):
        c = pltpu.make_async_copy(src, dst, sems.at[len(copies)])
        c.start()
        copies.append(c)

    for wire, at in ((up_ref, atom_dev - HALO), (down_ref, 0)):
        for s in range(samples):
            copy(atoms_ref.at[s, pl.ds(at, HALO)], wire.at[pl.ds(s * HALO, HALO)])
        copy(cond_ref.at[pl.ds(at, HALO)], wire.at[pl.ds(samples * HALO, HALO)])
    rows = (samples + 1) * HALO
    for wire, w, i in ((up_ref, windows - 1, query_len - EDGE_Q), (down_ref, 0, 0)):
        for q in range(EDGE_Q):
            copy(pair_ref.at[w, i + q], wire.at[pl.ds(rows + q * channels, channels)])
    rows += EDGE_Q * channels
    device = lax.axis_index("atom")
    position = device * atom_dev + iota((1, atom_dev), 1)
    usable = jnp.where((mask_ref[...] == 1) & (position < count_ref[0]), 1.0, 0.0)
    own = (token_ref[...] - device * (atom_dev // ATOMS_PER_TOKEN)).astype(F32)
    for slot, at in ((0, atom_dev - 128), (1, 0)):
        flags = usable[:, at : at + 128]
        tokens = own[:, at : at + 128]
        row = iota((16, 128), 0)
        block = jnp.where(row == 0, flags, jnp.where(row == 1, tokens, 0.0))
        info_ref[slot] = block.astype(BF16)
    copy(info_ref.at[0], up_ref.at[pl.ds(rows, 16)])
    copy(info_ref.at[1], down_ref.at[pl.ds(rows, 16)])
    for c in copies:
        c.wait()


def pair_lhs(weight_ref, lhs_ref):
    heads, channels = weight_ref.shape
    wide = 16 * channels
    w = weight_ref[...]
    w = w - jnp.mean(w, -1, keepdims=True)
    spread = jnp.where(iota((channels, wide), 1) % channels == iota((channels, wide), 0), 1.0, 0.0)
    tiled = jnp.dot(w, spread, precision=lax.Precision.HIGHEST, preferred_element_type=F32)
    full = jnp.concatenate(
        [jnp.broadcast_to(tiled[h : h + 1], (16, wide)) for h in range(heads)], axis=0
    )
    shape = (16 * heads, wide)
    full = jnp.where(iota(shape, 1) // channels == iota(shape, 0) % 16, full, 0.0)
    high = full.astype(BF16)
    rest = full - high.astype(F32)
    mid = rest.astype(BF16)
    low = (rest - mid.astype(F32)).astype(BF16)
    shape = (wide, wide)
    mean = jnp.where(iota(shape, 0) // channels == iota(shape, 1) // channels, 1.0 / channels, 0.0)
    n = 16 * heads
    lhs_ref[0:wide] = mean.astype(BF16)
    lhs_ref[wide : wide + n] = high
    lhs_ref[wide + n : wide + 2 * n] = mid
    lhs_ref[wide + 2 * n : wide + 3 * n] = low


def pair_bias(x, lhs, queries, heads):
    rows = queries * 16
    n = 16 * heads
    keys = x.shape[1]
    out = dot(lhs, x)
    off = x.astype(F32) - out[0:256][:rows]
    square = off * off
    half = jnp.sum(square.reshape(queries, 2, 8, keys), axis=1).reshape(queries * 8, keys)
    shape = (queries, queries * 8)
    gather = jnp.where(iota(shape, 1) // 8 == iota(shape, 0), 1.0 / 16, 0.0).astype(BF16)
    high = half.astype(BF16)
    low = (half - high.astype(F32)).astype(BF16)
    spread = dot(gather, high) + dot(gather, low)
    rstd = lax.rsqrt(spread + EPS)
    sums = out[256 : 256 + n] + out[256 + n : 256 + 2 * n] + out[256 + 2 * n : 256 + 3 * n]
    return [sums[h * 16 : h * 16 + queries] * rstd for h in range(heads)]


def bias_kernel(weight_ref, pair_ref, bias_ref, lhs_out_ref, lhs_ref):
    heads = weight_ref.shape[0]

    @pl.when(pl.program_id(0) == 0)
    def _():
        pair_lhs(weight_ref, lhs_ref)
        lhs_out_ref[...] = lhs_ref[...]

    lhs = lhs_ref[...]
    for w in range(pair_ref.shape[0]):
        query_len = pair_ref.shape[1] // 16
        for c in range(query_len // 16):
            x = pair_ref[w, c * 256 : (c + 1) * 256]
            for h, b in enumerate(pair_bias(x, lhs, 16, heads)):
                bias_ref[w, h * query_len + c * 16 : h * query_len + c * 16 + 16] = b


def block_kernel(
    count_ref,
    mask_ref,
    token_ref,
    atoms_ref,
    cond_ref,
    left_ref,
    right_ref,
    bias_ref,
    lhs_ref,
    ada_w_ref,
    ada_b_ref,
    zero_w_ref,
    zero_b_ref,
    qkvg_ref,
    query_b_ref,
    out_w_ref,
    swiglu_ref,
    down_ref,
    token_w_ref,
    atoms_out_ref,
    tokens_out_ref,
    scale0,
    shift0,
    scale1,
    shift1,
    gate0,
    gate1,
    edge_bias,
    live_ref,
    onehot_ref,
    inverse_ref,
    q_ref,
    k_ref,
    v_ref,
    gate_ref,
    blend_ref,
):
    atom_dev, width = atoms_ref.shape[1:]
    windows, score_rows, key_len = bias_ref.shape
    query_len = atom_dev // windows
    heads = score_rows // query_len
    head_dim = width // heads
    margin = (key_len - query_len) // 2
    tok_dev = atom_dev // ATOMS_PER_TOKEN
    samples = pl.num_programs(0)
    sample = pl.program_id(0)
    ext = atom_dev + 2 * HALO
    rows = atom_dev + 2 * EDGE
    first = HALO - EDGE
    hidden = down_ref.shape[0]

    @pl.when(sample == 0)
    def _():
        at = 4 * HALO
        cond = jnp.concatenate(
            [left_ref[at : at + HALO], cond_ref[...], right_ref[at : at + HALO]], axis=0
        )
        norm = norm_rows(cond.astype(F32)).astype(BF16)
        adapt = dot(norm, ada_w_ref[0])
        scale0[...] = sigmoid(adapt[:, :width] + ada_b_ref[0:1])
        shift0[...] = adapt[:, width:]
        norm = norm[first : first + rows]
        adapt = dot(norm, ada_w_ref[1])
        scale1[...] = sigmoid(adapt[:, :width] + ada_b_ref[1:2])
        shift1[...] = adapt[:, width:]
        gate0[...] = sigmoid(dot(norm, zero_w_ref[0]) + zero_b_ref[0:1])
        gate1[...] = sigmoid(dot(norm, zero_w_ref[1]) + zero_b_ref[1:2])
        at += HALO
        for e, ref in enumerate((left_ref, right_ref)):
            x = ref[at : at + EDGE_Q * 16]
            x = jnp.concatenate([x, jnp.zeros_like(x)], axis=0)
            for h, b in enumerate(pair_bias(x, lhs_ref[...], 16, heads)):
                edge_bias[e, h * EDGE_Q : (h + 1) * EDGE_Q] = b[:EDGE_Q]
        at += EDGE_Q * 16
        device = lax.axis_index("atom")
        position = device * atom_dev + iota((1, atom_dev), 1)
        usable = jnp.where((mask_ref[...] == 1) & (position < count_ref[0]), 1.0, 0.0)
        own = (token_ref[...] - device * tok_dev).astype(F32)
        info_l = left_ref[at : at + 16].astype(F32)
        info_r = right_ref[at : at + 16].astype(F32)
        flags = jnp.concatenate([info_l[0:1], usable, info_r[0:1]], axis=1)
        tokens = jnp.concatenate(
            [info_l[1:2] - tok_dev, own, info_r[1:2] + tok_dev], axis=1
        )
        total = flags.shape[1]
        flags8 = jnp.broadcast_to(flags, (8, total))
        rolled = {}
        for w in range(-1, windows + 1):
            start = 128 + query_len * w - margin
            shift = start % 128
            if shift not in rolled:
                rolled[shift] = pltpu.roll(flags8, total - shift, 1)
            lane = start - shift
            row = rolled[shift][0:1, lane : lane + key_len]
            live_ref[w + 1 : w + 2] = jnp.where(row > 0.5, 0.0, MASKED)
        shift = 128 - EDGE
        flags = pltpu.roll(flags8, total - shift, 1)[0:1]
        tokens = pltpu.roll(jnp.broadcast_to(tokens, (8, total)), total - shift, 1)[0:1]
        lanes = onehot_ref.shape[1]
        slot = iota((tok_dev, lanes), 0).astype(F32)
        inside = iota((tok_dev, lanes), 1) < rows
        hit = (tokens[:, :lanes] == slot) & (flags[:, :lanes] > 0.5) & inside
        onehot = jnp.where(hit, 1.0, 0.0)
        onehot_ref[...] = onehot.astype(BF16)
        counts = jnp.sum(onehot, -1, keepdims=True)
        inverse_ref[...] = jnp.broadcast_to(1.0 / jnp.maximum(counts, 1.0), inverse_ref.shape)
        v_ref[:, width:] = jnp.ones((ext, width), BF16)

    at = pl.multiple_of(sample * HALO, 16)
    stream = jnp.concatenate(
        [left_ref[pl.ds(at, HALO)], atoms_ref[0], right_ref[pl.ds(at, HALO)]], axis=0
    ).astype(F32)
    attn_in = (norm_rows(stream) * scale0[...] + shift0[...]).astype(BF16)
    keyval = dot(attn_in, qkvg_ref[:, width : 3 * width])
    k_ref[...] = keyval[:, :width].astype(BF16)
    v_ref[:, :width] = keyval[:, width:].astype(BF16)
    inner = attn_in[first : first + rows]
    factor = head_dim ** (-0.5)
    queries = dot(inner, qkvg_ref[:, :width])
    q_ref[...] = (queries + query_b_ref[0:1]) * factor
    gate_ref[...] = sigmoid(dot(inner, qkvg_ref[:, 3 * width :]))

    lane_head = iota((1, width), 1) // head_dim

    def attend(q, keys_at, bias, live):
        n = q.shape[0]
        wide = jnp.concatenate(
            [jnp.where(lane_head == h, q, 0.0) for h in range(heads)], axis=0
        ).astype(BF16)
        scores = dot_t(wide, k_ref[keys_at : keys_at + key_len]) + (bias + live)
        top = jnp.max(scores, -1, keepdims=True)
        weights = jnp.exp(scores - top).astype(BF16)
        out = dot(weights, v_ref[keys_at : keys_at + key_len])
        pick = out[0:n]
        for h in range(1, heads):
            head = jnp.concatenate([lane_head, lane_head], axis=1)
            pick = jnp.where(head == h, out[h * n : (h + 1) * n], pick)
        return pick[:, :width] / pick[:, width:]

    for w in range(windows):
        r = EDGE + w * query_len
        got = attend(
            q_ref[r : r + query_len],
            HALO + w * query_len - margin,
            bias_ref[w],
            live_ref[w + 1 : w + 2],
        )
        blend_ref[r : r + query_len] = (got * gate_ref[r : r + query_len]).astype(BF16)
    for e in range(2):
        r = (EDGE - EDGE_Q, EDGE + atom_dev)[e]
        w = (-1, windows)[e]
        got = attend(
            q_ref[r : r + EDGE_Q],
            HALO + w * query_len - margin,
            edge_bias[e],
            live_ref[w + 1 : w + 2],
        )
        got = got * gate_ref[r : r + EDGE_Q]
        pad = jnp.zeros_like(got)
        both = jnp.concatenate([pad, got] if e == 0 else [got, pad], axis=0)
        b = (0, EDGE + atom_dev)[e]
        blend_ref[b : b + EDGE] = both.astype(BF16)

    after = (
        stream[first : first + rows] + gate0[...] * dot(blend_ref[...], out_w_ref[...])
    ).astype(BF16)
    after32 = after.astype(F32)
    trans_in = (norm_rows(after32) * scale1[...] + shift1[...]).astype(BF16)
    mixed = dot(trans_in, swiglu_ref[...])
    a = mixed[:, :hidden]
    units = (a * sigmoid(a) * mixed[:, hidden:]).astype(BF16)
    result = (after32 + gate1[...] * dot(units, down_ref[...])).astype(BF16)
    atoms_out_ref[0] = result[EDGE : EDGE + atom_dev]
    features = jnp.maximum(dot(result, token_w_ref[...]), 0.0).astype(BF16)
    totals = dot(onehot_ref[:, :rows], features)
    for c in range(0, totals.shape[1], 128):
        tokens_out_ref[0, :, c : c + 128] = (totals[:, c : c + 128] * inverse_ref[...]).astype(
            BF16
        )


def on_device(
    atoms_in,
    cond,
    pair,
    atom_mask,
    atom_count,
    atom_to_token,
    ada_weight,
    ada_bias,
    zero_weight,
    zero_bias,
    qkvg_weight,
    query_bias,
    pair_weight,
    out_weight,
    swiglu_weight,
    down_weight,
    token_weight,
):
    samples, atom_dev, width = atoms_in.shape
    windows, query_len, channels, key_len = pair.shape
    heads = pair_weight.shape[0]
    hidden = down_weight.shape[0]
    token_width = token_weight.shape[1]
    tok_dev = atom_dev // ATOMS_PER_TOKEN
    ext = atom_dev + 2 * HALO
    rows = atom_dev + 2 * EDGE
    mask = atom_mask.reshape(1, atom_dev)
    token = atom_to_token.reshape(1, atom_dev)
    smem = pl.BlockSpec(memory_space=pltpu.SMEM)
    anywhere = pl.BlockSpec(memory_space=pl.ANY)
    vmem = pl.BlockSpec(memory_space=pltpu.VMEM)

    wire_rows = (samples + 1) * HALO + EDGE_Q * channels + 16
    wire = jax.ShapeDtypeStruct((wire_rows, width), BF16)
    n_copies = 2 * (samples + 1 + EDGE_Q + 1)
    up, down = pl.pallas_call(
        pack_kernel,
        out_shape=(wire, wire),
        in_specs=[smem, vmem, vmem, anywhere, anywhere, anywhere],
        out_specs=(anywhere, anywhere),
        scratch_shapes=[pltpu.VMEM((2, 16, 128), BF16), pltpu.SemaphoreType.DMA((n_copies,))],
        name="pack",
    )(atom_count, mask, token, atoms_in, cond, pair)
    count = lax.axis_size("atom")
    to_right = [(i, i + 1) for i in range(count - 1)]
    to_left = [(i + 1, i) for i in range(count - 1)]
    left = lax.ppermute(up, "atom", to_right)
    right = lax.ppermute(down, "atom", to_left)

    lhs_shape = (16 * channels + 3 * 16 * heads, 16 * channels)
    per_step = 3
    bias, lhs = pl.pallas_call(
        bias_kernel,
        grid=(windows // per_step,),
        out_shape=(
            jax.ShapeDtypeStruct((windows, heads * query_len, key_len), F32),
            jax.ShapeDtypeStruct(lhs_shape, BF16),
        ),
        in_specs=[
            pl.BlockSpec((heads, channels), lambda i: (0, 0)),
            pl.BlockSpec((per_step, query_len * channels, key_len), lambda i: (i, 0, 0)),
        ],
        out_specs=(
            pl.BlockSpec((per_step, heads * query_len, key_len), lambda i: (i, 0, 0)),
            pl.BlockSpec(lhs_shape, lambda i: (0, 0)),
        ),
        scratch_shapes=[pltpu.VMEM(lhs_shape, BF16)],
        name="bias",
    )(pair_weight, pair.reshape(windows, query_len * channels, key_len))

    def whole(array):
        zeros = (0,) * array.ndim
        return pl.BlockSpec(array.shape, lambda s: zeros)

    weights = (
        ada_weight,
        ada_bias,
        zero_weight,
        zero_bias,
        qkvg_weight,
        query_bias.reshape(1, width),
        out_weight,
        swiglu_weight,
        down_weight,
        token_weight,
    )
    resident = (cond, left, right, bias, lhs) + weights
    return pl.pallas_call(
        block_kernel,
        grid=(samples,),
        out_shape=(
            jax.ShapeDtypeStruct((samples, atom_dev, width), BF16),
            jax.ShapeDtypeStruct((samples, tok_dev, token_width), BF16),
        ),
        in_specs=[
            smem,
            whole(mask),
            whole(token),
            pl.BlockSpec((1, atom_dev, width), lambda s: (s, 0, 0)),
        ]
        + [whole(a) for a in resident],
        out_specs=(
            pl.BlockSpec((1, atom_dev, width), lambda s: (s, 0, 0)),
            pl.BlockSpec((1, tok_dev, token_width), lambda s: (s, 0, 0)),
        ),
        scratch_shapes=[
            pltpu.VMEM((ext, width), F32),
            pltpu.VMEM((ext, width), F32),
            pltpu.VMEM((rows, width), F32),
            pltpu.VMEM((rows, width), F32),
            pltpu.VMEM((rows, width), F32),
            pltpu.VMEM((rows, width), F32),
            pltpu.VMEM((2, heads * EDGE_Q, key_len), F32),
            pltpu.VMEM((16, key_len), F32),
            pltpu.VMEM((tok_dev, 512), BF16),
            pltpu.VMEM((tok_dev, 128), F32),
            pltpu.VMEM((rows, width), F32),
            pltpu.VMEM((ext, width), BF16),
            pltpu.VMEM((ext, 2 * width), BF16),
            pltpu.VMEM((rows, width), F32),
            pltpu.VMEM((rows, width), BF16),
        ],
        compiler_params=pltpu.CompilerParams(dimension_semantics=("arbitrary",)),
        name="block",
    )(atom_count, mask, token, atoms_in, *resident)


def solution(mesh):
    in_specs = (
        P("struct", "atom", None),
        P(("struct", "atom"), None),
        P(("struct", "atom"), None, None, None),
        P(("struct", "atom")),
        P("struct"),
        P(("struct", "atom")),
        P(),
        P(),
        P(),
        P(),
        P(),
        P(),
        P(),
        P(),
        P(),
        P(),
        P(),
    )
    out_specs = (P("struct", "atom", None), P("struct", "atom", None))
    return jax.shard_map(
        on_device, mesh=mesh, in_specs=in_specs, out_specs=out_specs, check_vma=False
    )
```

```python
import functools

import jax
import jax.numpy as jnp
from jax import lax
from jax.experimental import pallas as pl
from jax.experimental.pallas import tpu as pltpu
from jax.sharding import PartitionSpec as P

ATOMS_PER_TOKEN = 8
EPS = 1e-05
HALO = 80
EDGE = 16
EDGE_Q = 8
MASKED = -1e30
BF16 = jnp.bfloat16
F32 = jnp.float32


def dot(a, b):
    return jnp.dot(a, b, preferred_element_type=F32)


def dot_t(a, b):
    return lax.dot_general(a, b, (((1,), (1,)), ((), ())), preferred_element_type=F32)


def norm_rows(x):
    center = jnp.mean(x, -1, keepdims=True)
    off = x - center
    spread = jnp.mean(jnp.square(off), -1, keepdims=True)
    return off * lax.rsqrt(spread + EPS)


def sigmoid(x):
    return 1.0 / (1.0 + jnp.exp(-x))


def iota(shape, dim):
    return lax.broadcasted_iota(jnp.int32, shape, dim)


def pack_kernel(
    count_ref,
    mask_hbm,
    token_hbm,
    atoms_ref,
    cond_ref,
    pair_ref,
    up_ref,
    down_ref,
    info_ref,
    mask_ref,
    token_ref,
    sems,
):
    samples, atom_dev, _ = atoms_ref.shape
    windows, pair_rows, _ = pair_ref.shape
    edge_rows = EDGE_Q * 16
    copies = []

    def copy(src, dst):
        c = pltpu.make_async_copy(src, dst, sems.at[len(copies)])
        c.start()
        copies.append(c)

    copy(mask_hbm, mask_ref)
    copy(token_hbm, token_ref)
    rows = (samples + 1) * HALO
    for wire, at, w, p in (
        (up_ref, atom_dev - HALO, windows - 1, pair_rows - edge_rows),
        (down_ref, 0, 0, 0),
    ):
        for s in range(samples):
            copy(atoms_ref.at[s, pl.ds(at, HALO)], wire.at[pl.ds(s * HALO, HALO)])
        copy(cond_ref.at[pl.ds(at, HALO)], wire.at[pl.ds(samples * HALO, HALO)])
        copy(pair_ref.at[w, pl.ds(p, edge_rows)], wire.at[pl.ds(rows, edge_rows)])
    rows += edge_rows
    device = lax.axis_index("atom")
    position = device * atom_dev + iota((1, atom_dev), 1)
    for c in copies[:2]:
        c.wait()
    mask = mask_ref[...].reshape(1, atom_dev)
    token = token_ref[...].reshape(1, atom_dev)
    usable = jnp.where((mask == 1) & (position < count_ref[0]), 1.0, 0.0)
    own = (token - device * (atom_dev // ATOMS_PER_TOKEN)).astype(F32)
    row = iota((16, atom_dev), 0)
    info = jnp.where(row == 0, usable, jnp.where(row == 1, own, 0.0))
    info_ref[...] = info
    up_ref[rows : rows + 16] = info[:, atom_dev - 128 :].astype(BF16)
    down_ref[rows : rows + 16] = info[:, :128].astype(BF16)
    for c in copies[2:]:
        c.wait()


def pair_lhs(weight_ref, lhs_ref):
    heads, channels = weight_ref.shape
    wide = 16 * channels
    w = weight_ref[...]
    w = w - jnp.mean(w, -1, keepdims=True)
    spread = jnp.where(iota((channels, wide), 1) % channels == iota((channels, wide), 0), 1.0, 0.0)
    tiled = jnp.dot(w, spread, precision=lax.Precision.HIGHEST, preferred_element_type=F32)
    full = jnp.concatenate(
        [jnp.broadcast_to(tiled[h : h + 1], (16, wide)) for h in range(heads)], axis=0
    )
    shape = (16 * heads, wide)
    full = jnp.where(iota(shape, 1) // channels == iota(shape, 0) % 16, full, 0.0)
    high = full.astype(BF16)
    rest = full - high.astype(F32)
    mid = rest.astype(BF16)
    low = (rest - mid.astype(F32)).astype(BF16)
    shape = (wide, wide)
    mean = jnp.where(iota(shape, 0) // channels == iota(shape, 1) // channels, 1.0 / channels, 0.0)
    n = 16 * heads
    lhs_ref[0:wide] = mean.astype(BF16)
    lhs_ref[wide : wide + n] = high
    lhs_ref[wide + n : wide + 2 * n] = mid
    lhs_ref[wide + 2 * n : wide + 3 * n] = low


def pair_bias(x, lhs, queries, heads):
    rows = queries * 16
    n = 16 * heads
    keys = x.shape[1]
    out = dot(lhs, x)
    off = x.astype(F32) - out[0:256][:rows]
    square = off * off
    half = jnp.sum(square.reshape(queries, 2, 8, keys), axis=1).reshape(queries * 8, keys)
    shape = (queries, queries * 8)
    gather = jnp.where(iota(shape, 1) // 8 == iota(shape, 0), 1.0 / 16, 0.0).astype(BF16)
    high = half.astype(BF16)
    low = (half - high.astype(F32)).astype(BF16)
    spread = dot(gather, high) + dot(gather, low)
    rstd = lax.rsqrt(spread + EPS)
    sums = out[256 : 256 + n] + out[256 + n : 256 + 2 * n] + out[256 + 2 * n : 256 + 3 * n]
    return [sums[h * 16 : h * 16 + queries] * rstd for h in range(heads)]


def bias_kernel(weight_ref, pair_ref, bias_ref, lhs_ref):
    heads = weight_ref.shape[0]
    pair_lhs(weight_ref, lhs_ref)
    query_len = pair_ref.shape[1] // 16

    def window(w, carry):
        for c in range(query_len // 16):
            x = pair_ref[w, c * 256 : (c + 1) * 256]
            for h, b in enumerate(pair_bias(x, lhs_ref[...], 16, heads)):
                bias_ref[w, h * query_len + c * 16 : h * query_len + c * 16 + 16] = b
        return carry

    lax.fori_loop(0, pair_ref.shape[0], window, 0, unroll=3)


def block_kernel(
    atoms_ref,
    info_ref,
    cond_ref,
    left_ref,
    right_ref,
    bias_ref,
    lhs_ref,
    ada_w_ref,
    ada_b_ref,
    zero_w_ref,
    zero_b_ref,
    qkvg_ref,
    query_b_ref,
    out_w_ref,
    swiglu_ref,
    down_ref,
    token_w_ref,
    atoms_hbm,
    tokens_hbm,
    scale0,
    shift0,
    scale1,
    shift1,
    gate0,
    gate1,
    edge_bias,
    live_ref,
    onehot_ref,
    inverse_ref,
    q_ref,
    k_ref,
    v_ref,
    gate_ref,
    blend_ref,
    atoms_out_ref,
    tokens_out_ref,
    sems,
):
    samples, atom_dev, width = atoms_ref.shape
    windows, score_rows, key_len = bias_ref.shape
    query_len = atom_dev // windows
    heads = score_rows // query_len
    head_dim = width // heads
    margin = (key_len - query_len) // 2
    tok_dev = atom_dev // ATOMS_PER_TOKEN
    ext = atom_dev + 2 * HALO
    rows = atom_dev + 2 * EDGE
    first = HALO - EDGE
    hidden = down_ref.shape[0]

    at = 4 * HALO
    cond = jnp.concatenate(
        [left_ref[at : at + HALO], cond_ref[...], right_ref[at : at + HALO]], axis=0
    )
    norm = norm_rows(cond.astype(F32)).astype(BF16)
    adapt = dot(norm, ada_w_ref[0])
    scale0[...] = sigmoid(adapt[:, :width] + ada_b_ref[0:1])
    shift0[...] = adapt[:, width:]
    norm = norm[first : first + rows]
    adapt = dot(norm, ada_w_ref[1])
    scale1[...] = sigmoid(adapt[:, :width] + ada_b_ref[1:2])
    shift1[...] = adapt[:, width:]
    gate0[...] = sigmoid(dot(norm, zero_w_ref[0]) + zero_b_ref[0:1])
    gate1[...] = sigmoid(dot(norm, zero_w_ref[1]) + zero_b_ref[1:2])
    at += HALO
    for e, ref in enumerate((left_ref, right_ref)):
        x = ref[at : at + EDGE_Q * 16]
        x = jnp.concatenate([x, jnp.zeros_like(x)], axis=0)
        for h, b in enumerate(pair_bias(x, lhs_ref[...], 16, heads)):
            edge_bias[e, h * EDGE_Q : (h + 1) * EDGE_Q] = b[:EDGE_Q]
    at += EDGE_Q * 16
    usable = info_ref[0:1]
    own = info_ref[1:2]
    info_l = left_ref[at : at + 16].astype(F32)
    info_r = right_ref[at : at + 16].astype(F32)
    flags = jnp.concatenate([info_l[0:1], usable, info_r[0:1]], axis=1)
    tokens = jnp.concatenate(
        [info_l[1:2] - tok_dev, own, info_r[1:2] + tok_dev], axis=1
    )
    total = flags.shape[1]
    flags8 = jnp.broadcast_to(flags, (8, total))
    rolled = {}
    for w in range(-1, windows + 1):
        start = 128 + query_len * w - margin
        shift = start % 128
        if shift not in rolled:
            rolled[shift] = pltpu.roll(flags8, total - shift, 1)
        lane = start - shift
        row = rolled[shift][0:1, lane : lane + key_len]
        live_ref[w + 1 : w + 2] = jnp.where(row > 0.5, 0.0, MASKED)
    shift = 128 - EDGE
    flags = pltpu.roll(flags8, total - shift, 1)[0:1]
    tokens = pltpu.roll(jnp.broadcast_to(tokens, (8, total)), total - shift, 1)[0:1]
    lanes = onehot_ref.shape[1]
    slot = iota((tok_dev, lanes), 0).astype(F32)
    inside = iota((tok_dev, lanes), 1) < rows
    hit = (tokens[:, :lanes] == slot) & (flags[:, :lanes] > 0.5) & inside
    onehot = jnp.where(hit, 1.0, 0.0)
    onehot_ref[...] = onehot.astype(BF16)
    counts = jnp.sum(onehot, -1, keepdims=True)
    inverse_ref[...] = jnp.broadcast_to(1.0 / jnp.maximum(counts, 1.0), inverse_ref.shape)
    v_ref[:, width:] = jnp.ones((ext, width), BF16)

    lane_head = iota((1, width), 1) // head_dim

    def attend(q, keys_at, bias, live):
        n = q.shape[0]
        wide = jnp.concatenate(
            [jnp.where(lane_head == h, q, 0.0) for h in range(heads)], axis=0
        ).astype(BF16)
        scores = dot_t(wide, k_ref[keys_at : keys_at + key_len]) + (bias + live)
        top = jnp.max(scores, -1, keepdims=True)
        weights = jnp.exp(scores - top).astype(BF16)
        out = dot(weights, v_ref[keys_at : keys_at + key_len])
        pick = out[0:n]
        for h in range(1, heads):
            head = jnp.concatenate([lane_head, lane_head], axis=1)
            pick = jnp.where(head == h, out[h * n : (h + 1) * n], pick)
        return pick[:, :width] / pick[:, width:]

    def out_copies(sample):
        return (
            pltpu.make_async_copy(
                atoms_out_ref.at[sample], atoms_hbm.at[sample], sems.at[0, sample]
            ),
            pltpu.make_async_copy(
                tokens_out_ref.at[sample], tokens_hbm.at[sample], sems.at[1, sample]
            ),
        )

    def one_sample(sample, carry):
        at = pl.multiple_of(sample * HALO, 16)
        stream = jnp.concatenate(
            [left_ref[pl.ds(at, HALO)], atoms_ref[sample], right_ref[pl.ds(at, HALO)]], axis=0
        ).astype(F32)
        attn_in = (norm_rows(stream) * scale0[...] + shift0[...]).astype(BF16)
        keyval = dot(attn_in, qkvg_ref[:, width : 3 * width])
        k_ref[...] = keyval[:, :width].astype(BF16)
        v_ref[:, :width] = keyval[:, width:].astype(BF16)
        inner = attn_in[first : first + rows]
        factor = head_dim ** (-0.5)
        queries = dot(inner, qkvg_ref[:, :width])
        q_ref[...] = (queries + query_b_ref[0:1]) * factor
        gate_ref[...] = sigmoid(dot(inner, qkvg_ref[:, 3 * width :]))

        for w in range(windows):
            r = EDGE + w * query_len
            got = attend(
                q_ref[r : r + query_len],
                HALO + w * query_len - margin,
                bias_ref[w],
                live_ref[w + 1 : w + 2],
            )
            blend_ref[r : r + query_len] = (got * gate_ref[r : r + query_len]).astype(BF16)
        for e in range(2):
            r = (EDGE - EDGE_Q, EDGE + atom_dev)[e]
            w = (-1, windows)[e]
            got = attend(
                q_ref[r : r + EDGE_Q],
                HALO + w * query_len - margin,
                edge_bias[e],
                live_ref[w + 1 : w + 2],
            )
            got = got * gate_ref[r : r + EDGE_Q]
            pad = jnp.zeros_like(got)
            both = jnp.concatenate([pad, got] if e == 0 else [got, pad], axis=0)
            b = (0, EDGE + atom_dev)[e]
            blend_ref[b : b + EDGE] = both.astype(BF16)

        after = (
            stream[first : first + rows] + gate0[...] * dot(blend_ref[...], out_w_ref[...])
        ).astype(BF16)
        after32 = after.astype(F32)
        trans_in = (norm_rows(after32) * scale1[...] + shift1[...]).astype(BF16)
        mixed = dot(trans_in, swiglu_ref[...])
        a = mixed[:, :hidden]
        units = (a * sigmoid(a) * mixed[:, hidden:]).astype(BF16)
        result = (after32 + gate1[...] * dot(units, down_ref[...])).astype(BF16)
        atoms_out_ref[sample] = result[EDGE : EDGE + atom_dev]
        features = jnp.maximum(dot(result, token_w_ref[...]), 0.0).astype(BF16)
        totals = dot(onehot_ref[:, :rows], features)
        for c in range(0, totals.shape[1], 128):
            tokens_out_ref[sample, :, c : c + 128] = (totals[:, c : c + 128] * inverse_ref[...]).astype(
                BF16
            )
        for c in out_copies(sample):
            c.start()
        return carry

    lax.fori_loop(0, samples, one_sample, 0)
    for sample in range(samples):
        for c in out_copies(sample):
            c.wait()


def on_device(
    atoms_in,
    cond,
    pair,
    atom_mask,
    atom_count,
    atom_to_token,
    ada_weight,
    ada_bias,
    zero_weight,
    zero_bias,
    qkvg_weight,
    query_bias,
    pair_weight,
    out_weight,
    swiglu_weight,
    down_weight,
    token_weight,
):
    samples, atom_dev, width = atoms_in.shape
    windows, query_len, channels, key_len = pair.shape
    heads = pair_weight.shape[0]
    hidden = down_weight.shape[0]
    token_width = token_weight.shape[1]
    tok_dev = atom_dev // ATOMS_PER_TOKEN
    ext = atom_dev + 2 * HALO
    rows = atom_dev + 2 * EDGE
    smem = pl.BlockSpec(memory_space=pltpu.SMEM)
    far = pl.BlockSpec(memory_space=pltpu.HBM)
    vmem = pl.BlockSpec(memory_space=pltpu.VMEM)

    def near(array):
        return pltpu.with_memory_space_constraint(array, pltpu.VMEM)

    def away(array):
        return pltpu.with_memory_space_constraint(array, pltpu.HBM)

    wire_rows = (samples + 1) * HALO + EDGE_Q * channels + 16
    wire = pltpu.VMEM((wire_rows, width), BF16)
    pair = pair.reshape(windows, query_len * channels, key_len)
    up, down, info = pl.pallas_call(
        pack_kernel,
        out_shape=(wire, wire, pltpu.VMEM((16, atom_dev), F32)),
        in_specs=[smem] + [far] * 5,
        out_specs=(vmem, vmem, vmem),
        scratch_shapes=[
            pltpu.VMEM((atom_dev,), jnp.int32),
            pltpu.VMEM((atom_dev,), jnp.int32),
            pltpu.SemaphoreType.DMA((2 * (samples + 3),)),
        ],
        compiler_params=pltpu.CompilerParams(vmem_limit_bytes=4 << 20),
        name="pack",
    )(atom_count, *[away(a) for a in (atom_mask, atom_to_token, atoms_in, cond, pair)])
    count = lax.axis_size("atom")
    to_right = [(i, i + 1) for i in range(count - 1)]
    to_left = [(i + 1, i) for i in range(count - 1)]
    left = lax.ppermute(up, "atom", to_right)
    right = lax.ppermute(down, "atom", to_left)

    lhs_shape = (16 * channels + 3 * 16 * heads, 16 * channels)
    bias, lhs = pl.pallas_call(
        bias_kernel,
        out_shape=(
            pltpu.VMEM((windows, heads * query_len, key_len), F32),
            pltpu.VMEM(lhs_shape, BF16),
        ),
        in_specs=[vmem, vmem],
        out_specs=(vmem, vmem),
        compiler_params=pltpu.CompilerParams(vmem_limit_bytes=8 << 20),
        name="bias",
    )(pair_weight, near(pair))

    weights = (
        ada_weight,
        ada_bias,
        zero_weight,
        zero_bias,
        qkvg_weight,
        query_bias.reshape(1, width),
        out_weight,
        swiglu_weight,
        down_weight,
        token_weight,
    )
    operands = (atoms_in, info, cond, left, right, bias, lhs) + weights
    return pl.pallas_call(
        block_kernel,
        out_shape=(
            jax.ShapeDtypeStruct((samples, atom_dev, width), BF16),
            jax.ShapeDtypeStruct((samples, tok_dev, token_width), BF16),
        ),
        in_specs=[vmem] * len(operands),
        out_specs=(far, far),
        scratch_shapes=[
            pltpu.VMEM((ext, width), F32),
            pltpu.VMEM((ext, width), F32),
            pltpu.VMEM((rows, width), F32),
            pltpu.VMEM((rows, width), F32),
            pltpu.VMEM((rows, width), F32),
            pltpu.VMEM((rows, width), F32),
            pltpu.VMEM((2, heads * EDGE_Q, key_len), F32),
            pltpu.VMEM((16, key_len), F32),
            pltpu.VMEM((tok_dev, 512), BF16),
            pltpu.VMEM((tok_dev, 128), F32),
            pltpu.VMEM((rows, width), F32),
            pltpu.VMEM((ext, width), BF16),
            pltpu.VMEM((ext, 2 * width), BF16),
            pltpu.VMEM((rows, width), F32),
            pltpu.VMEM((rows, width), BF16),
            pltpu.VMEM((samples, atom_dev, width), BF16),
            pltpu.VMEM((samples, tok_dev, token_width), BF16),
            pltpu.SemaphoreType.DMA((2, samples)),
        ],
        compiler_params=pltpu.CompilerParams(vmem_limit_bytes=24 << 20),
        name="block",
    )(*[near(a) for a in operands])


def solution(mesh):
    in_specs = (
        P("struct", "atom", None),
        P(("struct", "atom"), None),
        P(("struct", "atom"), None, None, None),
        P(("struct", "atom")),
        P("struct"),
        P(("struct", "atom")),
        P(),
        P(),
        P(),
        P(),
        P(),
        P(),
        P(),
        P(),
        P(),
        P(),
        P(),
    )
    out_specs = (P("struct", "atom", None), P("struct", "atom", None))
    return jax.shard_map(
        on_device, mesh=mesh, in_specs=in_specs, out_specs=out_specs, check_vma=False
    )
```

```python
import functools

import jax
import jax.numpy as jnp
from jax import lax
from jax.experimental import pallas as pl
from jax.experimental.pallas import tpu as pltpu
from jax.sharding import PartitionSpec as P

ATOMS_PER_TOKEN = 8
EPS = 1e-05
HALO = 80
EDGE = 16
EDGE_Q = 8
MASKED = -1e30
BF16 = jnp.bfloat16
F32 = jnp.float32


def dot(a, b):
    return jnp.dot(a, b, preferred_element_type=F32)


def dot_t(a, b):
    return lax.dot_general(a, b, (((1,), (1,)), ((), ())), preferred_element_type=F32)


def norm_rows(x):
    center = jnp.mean(x, -1, keepdims=True)
    off = x - center
    spread = jnp.mean(jnp.square(off), -1, keepdims=True)
    return off * lax.rsqrt(spread + EPS)


def sigmoid(x):
    return 0.5 * jnp.tanh(0.5 * x) + 0.5


def iota(shape, dim):
    return lax.broadcasted_iota(jnp.int32, shape, dim)


def pack_kernel(
    count_ref,
    mask_hbm,
    token_hbm,
    atoms_ref,
    cond_ref,
    pair_ref,
    across_ref,
    within_ref,
    info_ref,
    mask_ref,
    token_ref,
    sems,
):
    samples, atom_dev, _ = atoms_ref.shape
    windows, pair_rows, _ = pair_ref.shape
    edge_rows = EDGE_Q * 16
    copies = []

    def copy(src, dst):
        c = pltpu.make_async_copy(src, dst, sems.at[len(copies)])
        c.start()
        copies.append(c)

    copy(mask_hbm, mask_ref)
    copy(token_hbm, token_ref)
    rows = (samples + 1) * HALO
    device = lax.axis_index("atom")
    odd = device % 2
    for wire, last in ((across_ref, odd), (within_ref, 1 - odd)):
        at = pl.multiple_of(last * (atom_dev - HALO), 16)
        w = last * (windows - 1)
        p = pl.multiple_of(last * (pair_rows - edge_rows), 16)
        for s in range(samples):
            copy(atoms_ref.at[s, pl.ds(at, HALO)], wire.at[pl.ds(s * HALO, HALO)])
        copy(cond_ref.at[pl.ds(at, HALO)], wire.at[pl.ds(samples * HALO, HALO)])
        copy(pair_ref.at[w, pl.ds(p, edge_rows)], wire.at[pl.ds(rows, edge_rows)])
    rows += edge_rows
    position = device * atom_dev + iota((1, atom_dev), 1)
    for c in copies[:2]:
        c.wait()
    mask = mask_ref[...].reshape(1, atom_dev)
    token = token_ref[...].reshape(1, atom_dev)
    usable = jnp.where((mask == 1) & (position < count_ref[0]), 1.0, 0.0)
    own = (token - device * (atom_dev // ATOMS_PER_TOKEN)).astype(F32)
    row = iota((16, atom_dev), 0)
    info = jnp.where(row == 0, usable, jnp.where(row == 1, own, 0.0))
    info_ref[...] = info
    end = info[:, atom_dev - 128 :]
    start = info[:, :128]
    across_ref[rows : rows + 16] = jnp.where(odd == 1, end, start).astype(BF16)
    within_ref[rows : rows + 16] = jnp.where(odd == 1, start, end).astype(BF16)
    for c in copies[2:]:
        c.wait()


def pair_lhs(weight_ref, lhs_ref):
    heads, channels = weight_ref.shape
    wide = 16 * channels
    w = weight_ref[...]
    w = w - jnp.mean(w, -1, keepdims=True)
    spread = jnp.where(iota((channels, wide), 1) % channels == iota((channels, wide), 0), 1.0, 0.0)
    tiled = jnp.dot(w, spread, precision=lax.Precision.HIGHEST, preferred_element_type=F32)
    full = jnp.concatenate(
        [jnp.broadcast_to(tiled[h : h + 1], (16, wide)) for h in range(heads)], axis=0
    )
    shape = (16 * heads, wide)
    full = jnp.where(iota(shape, 1) // channels == iota(shape, 0) % 16, full, 0.0)
    high = full.astype(BF16)
    rest = full - high.astype(F32)
    mid = rest.astype(BF16)
    low = (rest - mid.astype(F32)).astype(BF16)
    shape = (wide, wide)
    mean = jnp.where(iota(shape, 0) // channels == iota(shape, 1) // channels, 1.0 / channels, 0.0)
    n = 16 * heads
    lhs_ref[0:wide] = mean.astype(BF16)
    lhs_ref[wide : wide + n] = high
    lhs_ref[wide + n : wide + 2 * n] = mid
    lhs_ref[wide + 2 * n : wide + 3 * n] = low


def pair_sums(x, lhs, heads):
    n = 16 * heads
    out = dot(lhs, x)
    off = x.astype(F32) - out[0:256]
    square = off * off
    half = jnp.sum(square.reshape(16, 2, 8, -1), axis=1).reshape(128, -1)
    high = half.astype(BF16)
    low = (half - high.astype(F32)).astype(BF16)
    sums = out[256 : 256 + n] + out[256 + n : 256 + 2 * n] + out[256 + 2 * n : 256 + 3 * n]
    return sums, high, low


def pair_scale(sums, high, low):
    gather = jnp.where(iota((16, 128), 1) // 8 == iota((16, 128), 0), 1.0 / 16, 0.0).astype(BF16)
    rstd = lax.rsqrt(dot(gather, high) + dot(gather, low) + EPS)
    return sums * jnp.concatenate([rstd] * (sums.shape[0] // 16), axis=0)


def live_rows(flags, wanted, query_len, key_len, live_ref):
    total = flags.shape[1]
    flags8 = jnp.broadcast_to(flags, (8, total))
    rolled = {}
    for n, w in wanted:
        start = 128 + query_len * w - (key_len - query_len) // 2
        shift = start % 128
        if shift not in rolled:
            rolled[shift] = pltpu.roll(flags8, total - shift, 1)
        row = rolled[shift][0:1, start - shift : start - shift + key_len]
        live_ref[n : n + 1] = jnp.where(row > 0.5, 0.0, MASKED)


def bias_kernel(weight_ref, info_ref, pair_ref, bias_ref, lhs_ref, sum_ref, half_ref, live_ref):
    heads = weight_ref.shape[0]
    windows, score_rows, key_len = bias_ref.shape
    query_len = score_rows // heads
    pair_lhs(weight_ref, lhs_ref)
    ones = jnp.ones((1, 128), F32)
    flags = jnp.concatenate([ones, info_ref[0:1], ones], axis=1)
    live_rows(flags, [(w, w) for w in range(windows)], query_len, key_len, live_ref)
    per = query_len // 16
    n = 16 * heads

    def first(c):
        x = pair_ref[c // per, c % per * 256 : c % per * 256 + 256]
        sum_ref[c % 4], half_ref[c % 4, 0], half_ref[c % 4, 1] = pair_sums(
            x, lhs_ref[...], heads
        )

    def second(c):
        got = pair_scale(sum_ref[c % 4], half_ref[c % 4, 0], half_ref[c % 4, 1])
        w = c // per
        live = live_ref[w : w + 1]
        for h in range(heads):
            at = h * query_len + c % per * 16
            bias_ref[w, at : at + 16] = got[h * 16 : h * 16 + 16] + live

    chunks = range(windows * per)
    weave(
        skew([lambda c=c: first(c) for c in chunks], [lambda c=c: second(c) for c in chunks])
    )


PIECES = 4


def weave(*streams):
    steps = [x for x in streams if x]
    total = max(len(x) for x in steps)
    done = [0] * len(steps)
    for t in range(total):
        for n, x in enumerate(steps):
            while done[n] * total < (t + 1) * len(x) and done[n] < len(x):
                x[done[n]]()
                done[n] += 1


def skew(*stages):
    pieces = len(stages[0])
    out = []
    for t in range(pieces + len(stages) - 1):
        for n, stage in enumerate(stages):
            if 0 <= t - n < pieces:
                out.append(stage[t - n])
    return out


def block_kernel(
    atoms_ref,
    info_ref,
    cond_ref,
    across_ref,
    within_ref,
    bias_ref,
    lhs_ref,
    ada_w_ref,
    ada_b_ref,
    zero_w_ref,
    zero_b_ref,
    qkvg_ref,
    query_b_ref,
    out_w_ref,
    swiglu_ref,
    down_ref,
    token_w_ref,
    atoms_hbm,
    tokens_hbm,
    scale0,
    shift0,
    scale1,
    shift1,
    gate0,
    gate1,
    edge_bias,
    live_ref,
    onehot_ref,
    inverse_ref,
    left_ref,
    right_ref,
    norm_ref,
    wqg_ref,
    attn_ref,
    q_ref,
    k_ref,
    v_ref,
    gate_ref,
    score_ref,
    prob_ref,
    blend_ref,
    after_ref,
    trans_ref,
    hidden_ref,
    result_ref,
    feature_ref,
    tokens_ref,
    sems,
):
    samples, atom_dev, width = atoms_ref.shape
    windows, score_rows, key_len = bias_ref.shape
    query_len = atom_dev // windows
    heads = score_rows // query_len
    head_dim = width // heads
    margin = (key_len - query_len) // 2
    tok_dev = atom_dev // ATOMS_PER_TOKEN
    ext = atom_dev + 2 * HALO
    rows = atom_dev + 2 * EDGE
    first = HALO - EDGE
    hidden = down_ref.shape[0]
    token_width = token_w_ref.shape[1]
    factor = head_dim ** (-0.5)

    odd = lax.axis_index("atom") % 2 == 1
    left_ref[...] = jnp.where(odd, within_ref[...], across_ref[...])
    right_ref[...] = jnp.where(odd, across_ref[...], within_ref[...])
    at = samples * HALO
    wqg_ref[:, :width] = qkvg_ref[:, :width]
    wqg_ref[:, width:] = qkvg_ref[:, 3 * width :]
    at += HALO + EDGE_Q * 16
    usable = info_ref[0:1]
    own = info_ref[1:2]
    info_l = left_ref[at : at + 16].astype(F32)
    info_r = right_ref[at : at + 16].astype(F32)
    flags = jnp.concatenate([info_l[0:1], usable, info_r[0:1]], axis=1)
    tokens = jnp.concatenate([info_l[1:2] - tok_dev, own, info_r[1:2] + tok_dev], axis=1)
    total = flags.shape[1]
    halo = jnp.concatenate([info_l[0:1], jnp.ones_like(usable), info_r[0:1]], axis=1)
    inner = [(w + 1, w) for w in (0, 1, windows - 2, windows - 1)]
    live_rows(halo, inner, query_len, key_len, live_ref)
    outer = [(w + 1, w) for w in (-1, windows)]
    live_rows(flags, outer, query_len, key_len, live_ref)
    flags8 = jnp.broadcast_to(flags, (8, total))
    shift = 128 - EDGE
    flags = pltpu.roll(flags8, total - shift, 1)[0:1]
    tokens = pltpu.roll(jnp.broadcast_to(tokens, (8, total)), total - shift, 1)[0:1]
    lanes = onehot_ref.shape[1]
    slot = iota((tok_dev, lanes), 0).astype(F32)
    inside = iota((tok_dev, lanes), 1) < rows
    hit = (tokens[:, :lanes] == slot) & (flags[:, :lanes] > 0.5) & inside
    onehot = jnp.where(hit, 1.0, 0.0)
    onehot_ref[...] = onehot.astype(BF16)
    counts = jnp.sum(onehot, -1, keepdims=True)
    inverse_ref[...] = jnp.broadcast_to(1.0 / jnp.maximum(counts, 1.0), inverse_ref.shape)
    v_ref[:, :, width:] = jnp.ones((samples, ext, width), BF16)

    lane_head = iota((1, width), 1) // head_dim
    masks = [jnp.where(lane_head == h, 1.0, 0.0).astype(BF16) for h in range(heads)]
    pick_head = jnp.concatenate([lane_head, lane_head], axis=1)
    places = [
        (EDGE + w * query_len, query_len, HALO + w * query_len - margin, w)
        for w in range(windows)
    ]
    for w, r in ((-1, EDGE - EDGE_Q), (windows, EDGE + atom_dev)):
        places.append((r, EDGE_Q, HALO + w * query_len - margin, w))

    def spliced(middle, off, lo, hi):
        parts = []
        for base, size, ref, start in (
            (0, HALO, left_ref, off),
            (HALO, atom_dev, middle, 0),
            (HALO + atom_dev, HALO, right_ref, off),
        ):
            x, y = max(lo, base), min(hi, base + size)
            if x < y:
                parts.append(ref[x - base + start : y - base + start])
        return parts[0] if len(parts) == 1 else jnp.concatenate(parts, axis=0)

    def stream_rows(s, lo, hi):
        return spliced(atoms_ref.at[s], s * HALO, lo, hi)

    def each(step, n, pieces):
        size = -(-n // pieces // 16) * 16
        return [
            lambda lo=lo, hi=min(n, lo + size): step(lo, hi) for lo in range(0, n, size)
        ]

    def cond_piece(lo, hi):
        x = spliced(cond_ref, samples * HALO, lo, hi).astype(F32)
        norm = norm_rows(x).astype(BF16)
        norm_ref[lo:hi] = norm
        adapt = dot(norm, ada_w_ref[0])
        scale0[lo:hi] = sigmoid(adapt[:, :width] + ada_b_ref[0:1])
        shift0[lo:hi] = adapt[:, width:]

    def gates():
        def adapt_piece(lo, hi):
            adapt = dot(norm_ref[first + lo : first + hi], ada_w_ref[1])
            scale1[lo:hi] = sigmoid(adapt[:, :width] + ada_b_ref[1:2])
            shift1[lo:hi] = adapt[:, width:]

        def zero_piece(lo, hi):
            norm = norm_ref[first + lo : first + hi]
            gate0[lo:hi] = sigmoid(dot(norm, zero_w_ref[0]) + zero_b_ref[0:1])
            gate1[lo:hi] = sigmoid(dot(norm, zero_w_ref[1]) + zero_b_ref[1:2])

        def edge_piece(e):
            x = (left_ref, right_ref)[e]
            start = (samples + 1) * HALO
            x = x[start : start + EDGE_Q * 16]
            x = jnp.concatenate([x, jnp.zeros_like(x)], axis=0)
            got = pair_scale(*pair_sums(x, lhs_ref[...], heads))
            for h in range(heads):
                edge_bias[e, h * EDGE_Q : (h + 1) * EDGE_Q] = got[h * 16 : h * 16 + EDGE_Q]

        out = [lambda e=e: edge_piece(e) for e in range(2)]
        return out + skew(each(adapt_piece, rows, 4), each(zero_piece, rows, 4))

    def prepare(s):
        def norm_piece(lo, hi):
            x = stream_rows(s, lo, hi).astype(F32)
            y = norm_rows(x) * scale0[lo:hi] + shift0[lo:hi]
            attn_ref[s, lo:hi] = y.astype(BF16)

        def keyval_piece(lo, hi):
            y = dot(attn_ref[s, lo:hi], qkvg_ref[:, width : 3 * width])
            k_ref[s, lo:hi] = y[:, :width].astype(BF16)
            v_ref[s, lo:hi, :width] = y[:, width:].astype(BF16)

        def query_piece(lo, hi):
            lo, hi = max(lo - first, 0), min(hi - first, rows)
            y = dot(attn_ref[s, first + lo : first + hi], wqg_ref[...])
            q_ref[s, lo:hi] = ((y[:, :width] + query_b_ref[0:1]) * factor).astype(BF16)
            gate_ref[s, lo:hi] = sigmoid(y[:, width:])

        stages = [each(f, ext, 4) for f in (norm_piece, keyval_piece, query_piece)]
        if s == 0:
            stages = [each(cond_piece, ext, 4)] + stages
        return skew(*stages)

    def attend(s):
        def score(t):
            r, n, key, w = places[t]
            if n >= 16:
                q = q_ref[s, r : r + n]
                wide = jnp.concatenate([q * masks[h] for h in range(heads)], axis=0)
                bias = bias_ref[w]
            else:
                base = r // 16 * 16
                q = q_ref[s, base : base + 16].astype(F32)[r - base : r - base + n]
                wide = jnp.concatenate(
                    [jnp.where(lane_head == h, q, 0.0) for h in range(heads)], axis=0
                ).astype(BF16)
                bias = edge_bias[0 if w < 0 else 1]
            got = dot_t(wide, k_ref[s, key : key + key_len])
            if 1 < w < windows - 2:
                got = got + bias
            else:
                got = got + (bias + live_ref[w + 1 : w + 2])
            score_ref[s % 2, t, : heads * n] = got

        def soften(t):
            n = heads * places[t][1]
            x = score_ref[s % 2, t, :n]
            top = jnp.max(x, -1, keepdims=True)
            prob_ref[s % 2, t, :n] = jnp.exp(x - top).astype(BF16)

        def blend(t):
            r, n, key, w = places[t]
            out = dot(prob_ref[s % 2, t, : heads * n], v_ref[s, key : key + key_len])
            pick = out[0:n]
            for h in range(1, heads):
                pick = jnp.where(pick_head == h, out[h * n : (h + 1) * n], pick)
            got = pick[:, :width] / pick[:, width:] * gate_ref[s, r : r + n]
            if n < 16:
                pad = jnp.zeros_like(got)
                base = r // 16 * 16
                got = jnp.concatenate([pad, got] if r > base else [got, pad], axis=0)
                r, n = base, 16
            blend_ref[s, r : r + n] = got.astype(BF16)

        count = len(places)
        out = []
        for t in range(count + 2):
            if t < count:
                out.append(lambda t=t: score(t))
            if 0 <= t - 1 < count:
                out.append(lambda t=t: soften(t - 1))
            if 0 <= t - 2 < count:
                out.append(lambda t=t: blend(t - 2))
        return out

    def out_copies(s):
        return (
            pltpu.make_async_copy(
                result_ref.at[s, pl.ds(EDGE, atom_dev)], atoms_hbm.at[s], sems.at[0, s]
            ),
            pltpu.make_async_copy(tokens_ref.at[s], tokens_hbm.at[s], sems.at[1, s]),
        )

    def finish(s):
        def after_piece(lo, hi):
            x = stream_rows(s, first + lo, first + hi).astype(F32)
            y = (x + gate0[lo:hi] * dot(blend_ref[s, lo:hi], out_w_ref[...])).astype(BF16)
            after_ref[s, lo:hi] = y
            z = norm_rows(y.astype(F32)) * scale1[lo:hi] + shift1[lo:hi]
            trans_ref[s, lo:hi] = z.astype(BF16)

        def hidden_piece(lo, hi):
            y = dot(trans_ref[s, lo:hi], swiglu_ref[...])
            a = y[:, :hidden]
            hidden_ref[s, lo:hi] = (a * sigmoid(a) * y[:, hidden:]).astype(BF16)

        def result_piece(lo, hi):
            y = gate1[lo:hi] * dot(hidden_ref[s, lo:hi], down_ref[...])
            result_ref[s, lo:hi] = (after_ref[s, lo:hi].astype(F32) + y).astype(BF16)

        def feature_piece(lo, hi):
            y = dot(result_ref[s, lo:hi], token_w_ref[...])
            feature_ref[s % 2, lo:hi] = jnp.maximum(y, 0.0).astype(BF16)

        def token_piece(lo, hi):
            y = dot(onehot_ref[:, :rows], feature_ref[s % 2, :, lo:hi])
            for c in range(lo, hi, 128):
                z = y[:, c - lo : c - lo + 128] * inverse_ref[...]
                tokens_ref[s, :, c : c + 128] = z.astype(BF16)

        def send():
            for c in out_copies(s):
                c.start()

        stages = (after_piece, hidden_piece, result_piece, feature_piece)
        out = skew(*[each(f, rows, PIECES) for f in stages])
        out += [lambda lo=lo: token_piece(lo, lo + 256) for lo in range(0, token_width, 256)]
        return out + [send]

    weave(prepare(0))
    for s in range(samples):
        weave(
            attend(s),
            finish(s - 1) if s > 0 else gates(),
            prepare(s + 1) if s + 1 < samples else None,
        )
    weave(finish(samples - 1))
    for s in range(samples):
        for c in out_copies(s):
            c.wait()


def on_device(
    atoms_in,
    cond,
    pair,
    atom_mask,
    atom_count,
    atom_to_token,
    ada_weight,
    ada_bias,
    zero_weight,
    zero_bias,
    qkvg_weight,
    query_bias,
    pair_weight,
    out_weight,
    swiglu_weight,
    down_weight,
    token_weight,
):
    samples, atom_dev, width = atoms_in.shape
    windows, query_len, channels, key_len = pair.shape
    heads = pair_weight.shape[0]
    hidden = down_weight.shape[0]
    token_width = token_weight.shape[1]
    tok_dev = atom_dev // ATOMS_PER_TOKEN
    ext = atom_dev + 2 * HALO
    rows = atom_dev + 2 * EDGE
    smem = pl.BlockSpec(memory_space=pltpu.SMEM)
    far = pl.BlockSpec(memory_space=pltpu.HBM)
    vmem = pl.BlockSpec(memory_space=pltpu.VMEM)

    def near(array):
        return pltpu.with_memory_space_constraint(array, pltpu.VMEM)

    def away(array):
        return pltpu.with_memory_space_constraint(array, pltpu.HBM)

    wire_rows = (samples + 1) * HALO + EDGE_Q * channels + 16
    wire = pltpu.VMEM((wire_rows, width), BF16)
    pair = pair.reshape(windows, query_len * channels, key_len)
    across, within, info = pl.pallas_call(
        pack_kernel,
        out_shape=(wire, wire, pltpu.VMEM((16, atom_dev), F32)),
        in_specs=[smem] + [far] * 5,
        out_specs=(vmem, vmem, vmem),
        scratch_shapes=[
            pltpu.VMEM((atom_dev,), jnp.int32),
            pltpu.VMEM((atom_dev,), jnp.int32),
            pltpu.SemaphoreType.DMA((2 * (samples + 3),)),
        ],
        compiler_params=pltpu.CompilerParams(vmem_limit_bytes=4 << 20),
        name="pack",
    )(atom_count, *[away(a) for a in (atom_mask, atom_to_token, atoms_in, cond, pair)])
    count = lax.axis_size("atom")
    swaps = [[(i, i + 1) for i in range(at, count - 1, 2)] for at in (1, 0)]
    swaps = [pairs + [(j, i) for i, j in pairs] for pairs in swaps]
    across = lax.ppermute(across, "atom", swaps[0])
    within = lax.ppermute(within, "atom", swaps[1])

    lhs_shape = (16 * channels + 3 * 16 * heads, 16 * channels)
    bias, lhs = pl.pallas_call(
        bias_kernel,
        out_shape=(
            pltpu.VMEM((windows, heads * query_len, key_len), F32),
            pltpu.VMEM(lhs_shape, BF16),
        ),
        in_specs=[vmem] * 3,
        out_specs=(vmem, vmem),
        scratch_shapes=[
            pltpu.VMEM((4, 16 * heads, key_len), F32),
            pltpu.VMEM((4, 2, 128, key_len), BF16),
            pltpu.VMEM((16, key_len), F32),
        ],
        compiler_params=pltpu.CompilerParams(vmem_limit_bytes=8 << 20),
        name="bias",
    )(pair_weight, near(info), near(pair))

    weights = (
        ada_weight,
        ada_bias,
        zero_weight,
        zero_bias,
        qkvg_weight,
        query_bias.reshape(1, width),
        out_weight,
        swiglu_weight,
        down_weight,
        token_weight,
    )
    operands = (atoms_in, info, cond, across, within, bias, lhs) + weights
    return pl.pallas_call(
        block_kernel,
        out_shape=(
            jax.ShapeDtypeStruct((samples, atom_dev, width), BF16),
            jax.ShapeDtypeStruct((samples, tok_dev, token_width), BF16),
        ),
        in_specs=[vmem] * len(operands),
        out_specs=(far, far),
        scratch_shapes=[
            pltpu.VMEM((ext, width), F32),
            pltpu.VMEM((ext, width), F32),
            pltpu.VMEM((rows, width), F32),
            pltpu.VMEM((rows, width), F32),
            pltpu.VMEM((rows, width), F32),
            pltpu.VMEM((rows, width), F32),
            pltpu.VMEM((2, heads * EDGE_Q, key_len), F32),
            pltpu.VMEM((16, key_len), F32),
            pltpu.VMEM((tok_dev, 512), BF16),
            pltpu.VMEM((tok_dev, 128), F32),
            pltpu.VMEM((wire_rows, width), BF16),
            pltpu.VMEM((wire_rows, width), BF16),
            pltpu.VMEM((ext, width), BF16),
            pltpu.VMEM((width, 2 * width), BF16),
            pltpu.VMEM((samples, ext, width), BF16),
            pltpu.VMEM((samples, rows, width), BF16),
            pltpu.VMEM((samples, ext, width), BF16),
            pltpu.VMEM((samples, ext, 2 * width), BF16),
            pltpu.VMEM((samples, rows, width), F32),
            pltpu.VMEM((2, windows + 2, heads * query_len, key_len), F32),
            pltpu.VMEM((2, windows + 2, heads * query_len, key_len), BF16),
            pltpu.VMEM((samples, rows, width), BF16),
            pltpu.VMEM((samples, rows, width), BF16),
            pltpu.VMEM((samples, rows, width), BF16),
            pltpu.VMEM((samples, rows, hidden), BF16),
            pltpu.VMEM((samples, rows, width), BF16),
            pltpu.VMEM((2, rows, token_width), BF16),
            pltpu.VMEM((samples, tok_dev, token_width), BF16),
            pltpu.SemaphoreType.DMA((2, samples)),
        ],
        compiler_params=pltpu.CompilerParams(vmem_limit_bytes=24 << 20),
        name="block",
    )(*[near(a) for a in operands])


def solution(mesh):
    in_specs = (
        P("struct", "atom", None),
        P(("struct", "atom"), None),
        P(("struct", "atom"), None, None, None),
        P(("struct", "atom")),
        P("struct"),
        P(("struct", "atom")),
        P(),
        P(),
        P(),
        P(),
        P(),
        P(),
        P(),
        P(),
        P(),
        P(),
        P(),
    )
    out_specs = (P("struct", "atom", None), P("struct", "atom", None))
    return jax.shard_map(
        on_device, mesh=mesh, in_specs=in_specs, out_specs=out_specs, check_vma=False
    )
```

```python
import functools

import jax
import jax.numpy as jnp
from jax import lax
from jax.experimental import pallas as pl
from jax.experimental.pallas import tpu as pltpu
from jax.sharding import PartitionSpec as P

ATOMS_PER_TOKEN = 8
EPS = 1e-05
HALO = 80
EDGE = 16
EDGE_Q = 8
MASKED = -1e30
BF16 = jnp.bfloat16
F32 = jnp.float32


def dot(a, b):
    return jnp.dot(a, b, preferred_element_type=F32)


def dot_t(a, b):
    return lax.dot_general(a, b, (((1,), (1,)), ((), ())), preferred_element_type=F32)


def norm_rows(x):
    center = jnp.mean(x, -1, keepdims=True)
    off = x - center
    spread = jnp.mean(jnp.square(off), -1, keepdims=True)
    return off * lax.rsqrt(spread + EPS)


def sigmoid(x):
    return 0.5 * jnp.tanh(0.5 * x) + 0.5


def iota(shape, dim):
    return lax.broadcasted_iota(jnp.int32, shape, dim)


def pack_kernel(
    mask_hbm,
    token_hbm,
    atoms_ref,
    cond_ref,
    pair_ref,
    across_ref,
    within_ref,
    info_ref,
    mask_ref,
    token_ref,
    sems,
):
    samples, atom_dev, _ = atoms_ref.shape
    windows, pair_rows, _ = pair_ref.shape
    edge_rows = EDGE_Q * 16
    copies = []

    def copy(src, dst):
        c = pltpu.make_async_copy(src, dst, sems.at[len(copies)])
        c.start()
        copies.append(c)

    copy(mask_hbm, mask_ref)
    copy(token_hbm, token_ref)
    rows = (samples + 1) * HALO
    device = lax.axis_index("atom")
    odd = device % 2
    for wire, last in ((across_ref, odd), (within_ref, 1 - odd)):
        at = pl.multiple_of(last * (atom_dev - HALO), 16)
        w = last * (windows - 1)
        p = pl.multiple_of(last * (pair_rows - edge_rows), 16)
        for s in range(samples):
            copy(atoms_ref.at[s, pl.ds(at, HALO)], wire.at[pl.ds(s * HALO, HALO)])
        copy(cond_ref.at[pl.ds(at, HALO)], wire.at[pl.ds(samples * HALO, HALO)])
        copy(pair_ref.at[w, pl.ds(p, edge_rows)], wire.at[pl.ds(rows, edge_rows)])
    rows += edge_rows
    for c in copies[:2]:
        c.wait()
    mask = mask_ref[...].reshape(1, atom_dev)
    token = token_ref[...].reshape(1, atom_dev)
    exists = jnp.where(mask == 1, 1.0, 0.0)
    own = (token - device * (atom_dev // ATOMS_PER_TOKEN)).astype(F32)
    row = iota((16, atom_dev), 0)
    info = jnp.where(row == 0, exists, jnp.where(row == 1, own, 0.0))
    info_ref[...] = info
    end = info[:, atom_dev - 128 :]
    start = info[:, :128]
    across_ref[rows : rows + 16] = jnp.where(odd == 1, end, start).astype(BF16)
    within_ref[rows : rows + 16] = jnp.where(odd == 1, start, end).astype(BF16)
    for c in copies[2:]:
        c.wait()


def pair_lhs(weight_ref, lhs_ref):
    heads, channels = weight_ref.shape
    wide = 16 * channels
    w = weight_ref[...]
    w = w - jnp.mean(w, -1, keepdims=True)
    spread = jnp.where(iota((channels, wide), 1) % channels == iota((channels, wide), 0), 1.0, 0.0)
    tiled = jnp.dot(w, spread, precision=lax.Precision.HIGHEST, preferred_element_type=F32)
    full = jnp.concatenate(
        [jnp.broadcast_to(tiled[h : h + 1], (16, wide)) for h in range(heads)], axis=0
    )
    shape = (16 * heads, wide)
    full = jnp.where(iota(shape, 1) // channels == iota(shape, 0) % 16, full, 0.0)
    high = full.astype(BF16)
    rest = full - high.astype(F32)
    mid = rest.astype(BF16)
    low = (rest - mid.astype(F32)).astype(BF16)
    n = 16 * heads
    lhs_ref[0:n] = high
    lhs_ref[n : 2 * n] = mid
    lhs_ref[2 * n : 3 * n] = low


def pair_sums(x, lhs, heads):
    n = 16 * heads
    out = dot(lhs, x)
    rows = x.astype(F32).reshape(16, 16, -1)
    off = rows - jnp.mean(rows, axis=1, keepdims=True)
    square = off * off
    half = (square[:, :8] + square[:, 8:]).reshape(128, -1)
    high = half.astype(BF16)
    low = (half - high.astype(F32)).astype(BF16)
    sums = out[0:n] + out[n : 2 * n] + out[2 * n : 3 * n]
    return sums, high, low


def pair_scale(sums, high, low):
    gather = jnp.where(iota((16, 128), 1) // 8 == iota((16, 128), 0), 1.0 / 16, 0.0).astype(BF16)
    rstd = lax.rsqrt(dot(gather, high) + dot(gather, low) + EPS)
    return sums * jnp.concatenate([rstd] * (sums.shape[0] // 16), axis=0)


def usable_only(flags, start, atom_dev, count_ref):
    lanes = flags.shape[1]
    device = lax.axis_index("atom")
    position = device * atom_dev + start + iota((1, lanes), 1)
    count = jnp.broadcast_to(count_ref[0:1, 0:1], (1, lanes))
    return jnp.where(position < count, flags, 0.0)


def live_rows(flags, wanted, query_len, key_len, live_ref):
    total = flags.shape[1]
    flags8 = jnp.broadcast_to(flags, (8, total))
    rolled = {}
    for n, w in wanted:
        start = 128 + query_len * w - (key_len - query_len) // 2
        shift = start % 128
        if shift not in rolled:
            rolled[shift] = pltpu.roll(flags8, total - shift, 1)
        row = rolled[shift][0:1, start - shift : start - shift + key_len]
        live_ref[n : n + 1] = jnp.where(row > 0.5, 0.0, MASKED)


def bias_kernel(count_ref, weight_ref, info_ref, pair_ref, bias_ref, lhs_ref, sum_ref, half_ref, live_ref):
    heads = weight_ref.shape[0]
    windows, score_rows, key_len = bias_ref.shape
    query_len = score_rows // heads
    pair_lhs(weight_ref, lhs_ref)
    ones = jnp.ones((1, 128), F32)
    flags = jnp.concatenate([ones, usable_only(info_ref[0:1], 0, info_ref.shape[1], count_ref), ones], axis=1)
    live_rows(flags, [(w, w) for w in range(windows)], query_len, key_len, live_ref)
    per = query_len // 16
    n = 16 * heads

    def first(c):
        x = pair_ref[c // per, c % per * 256 : c % per * 256 + 256]
        sum_ref[c % 4], half_ref[c % 4, 0], half_ref[c % 4, 1] = pair_sums(
            x, lhs_ref[...], heads
        )

    def second(c):
        got = pair_scale(sum_ref[c % 4], half_ref[c % 4, 0], half_ref[c % 4, 1])
        w = c // per
        live = live_ref[w : w + 1]
        for h in range(heads):
            at = h * query_len + c % per * 16
            bias_ref[w, at : at + 16] = got[h * 16 : h * 16 + 16] + live

    chunks = range(windows * per)
    weave(
        skew([lambda c=c: first(c) for c in chunks], [lambda c=c: second(c) for c in chunks])
    )


PIECES = 4


def weave(*streams):
    steps = [x for x in streams if x]
    total = max(len(x) for x in steps)
    done = [0] * len(steps)
    for t in range(total):
        for n, x in enumerate(steps):
            while done[n] * total < (t + 1) * len(x) and done[n] < len(x):
                x[done[n]]()
                done[n] += 1


def skew(*stages):
    pieces = len(stages[0])
    out = []
    for t in range(pieces + len(stages) - 1):
        for n, stage in enumerate(stages):
            if 0 <= t - n < pieces:
                out.append(stage[t - n])
    return out


def block_kernel(
    atoms_ref,
    count_ref,
    info_ref,
    cond_ref,
    across_ref,
    within_ref,
    bias_ref,
    lhs_ref,
    ada_w_ref,
    ada_b_ref,
    zero_w_ref,
    zero_b_ref,
    qkvg_ref,
    query_b_ref,
    out_w_ref,
    swiglu_ref,
    down_ref,
    token_w_ref,
    atoms_hbm,
    tokens_hbm,
    scale0,
    shift0,
    scale1,
    shift1,
    gate0,
    gate1,
    edge_bias,
    live_ref,
    onehot_ref,
    inverse_ref,
    left_ref,
    right_ref,
    norm_ref,
    wqg_ref,
    attn_ref,
    q_ref,
    k_ref,
    v_ref,
    gate_ref,
    score_ref,
    prob_ref,
    total_ref,
    blend_ref,
    after_ref,
    trans_ref,
    hidden_ref,
    result_ref,
    feature_ref,
    tokens_ref,
    sems,
):
    samples, atom_dev, width = atoms_ref.shape
    windows, score_rows, key_len = bias_ref.shape
    query_len = atom_dev // windows
    heads = score_rows // query_len
    head_dim = width // heads
    margin = (key_len - query_len) // 2
    tok_dev = atom_dev // ATOMS_PER_TOKEN
    ext = atom_dev + 2 * HALO
    rows = atom_dev + 2 * EDGE
    first = HALO - EDGE
    hidden = down_ref.shape[0]
    token_width = token_w_ref.shape[1]
    factor = head_dim ** (-0.5)

    odd = lax.axis_index("atom") % 2 == 1
    left_ref[...] = jnp.where(odd, within_ref[...], across_ref[...])
    right_ref[...] = jnp.where(odd, across_ref[...], within_ref[...])
    at = samples * HALO
    wqg_ref[:, :width] = qkvg_ref[:, :width]
    wqg_ref[:, width:] = qkvg_ref[:, 3 * width :]
    at += HALO + EDGE_Q * 16
    exists = info_ref[0:1]
    own = info_ref[1:2]
    info_l = left_ref[at : at + 16].astype(F32)
    info_r = right_ref[at : at + 16].astype(F32)
    flags = jnp.concatenate([info_l[0:1], exists, info_r[0:1]], axis=1)
    flags = usable_only(flags, -128, atom_dev, count_ref)
    tokens = jnp.concatenate([info_l[1:2] - tok_dev, own, info_r[1:2] + tok_dev], axis=1)
    total = flags.shape[1]
    lane = iota((1, total), 1)
    halo = jnp.where((lane >= 128) & (lane < 128 + atom_dev), 1.0, flags)
    inner = [(w + 1, w) for w in (0, 1, windows - 2, windows - 1)]
    live_rows(halo, inner, query_len, key_len, live_ref)
    outer = [(w + 1, w) for w in (-1, windows)]
    live_rows(flags, outer, query_len, key_len, live_ref)
    flags8 = jnp.broadcast_to(flags, (8, total))
    shift = 128 - EDGE
    flags = pltpu.roll(flags8, total - shift, 1)[0:1]
    tokens = pltpu.roll(jnp.broadcast_to(tokens, (8, total)), total - shift, 1)[0:1]
    lanes = onehot_ref.shape[1]
    slot = iota((tok_dev, lanes), 0).astype(F32)
    inside = iota((tok_dev, lanes), 1) < rows
    hit = (tokens[:, :lanes] == slot) & (flags[:, :lanes] > 0.5) & inside
    onehot = jnp.where(hit, 1.0, 0.0)
    onehot_ref[...] = onehot.astype(BF16)
    counts = jnp.sum(onehot, -1, keepdims=True)
    inverse_ref[...] = jnp.broadcast_to(1.0 / jnp.maximum(counts, 1.0), inverse_ref.shape)

    lane_head = iota((1, width), 1) // head_dim
    masks = [jnp.where(lane_head == h, 1.0, 0.0).astype(BF16) for h in range(heads)]
    places = [
        (EDGE + w * query_len, query_len, HALO + w * query_len - margin, w)
        for w in range(windows)
    ]
    for w, r in ((-1, EDGE - EDGE_Q), (windows, EDGE + atom_dev)):
        places.append((r, EDGE_Q, HALO + w * query_len - margin, w))

    def spliced(middle, off, lo, hi):
        parts = []
        for base, size, ref, start in (
            (0, HALO, left_ref, off),
            (HALO, atom_dev, middle, 0),
            (HALO + atom_dev, HALO, right_ref, off),
        ):
            x, y = max(lo, base), min(hi, base + size)
            if x < y:
                parts.append(ref[x - base + start : y - base + start])
        return parts[0] if len(parts) == 1 else jnp.concatenate(parts, axis=0)

    def stream_rows(s, lo, hi):
        return spliced(atoms_ref.at[s], s * HALO, lo, hi)

    def each(step, n, pieces):
        size = -(-n // pieces // 16) * 16
        return [
            lambda lo=lo, hi=min(n, lo + size): step(lo, hi) for lo in range(0, n, size)
        ]

    def cond_piece(lo, hi):
        x = spliced(cond_ref, samples * HALO, lo, hi).astype(F32)
        norm = norm_rows(x).astype(BF16)
        norm_ref[lo:hi] = norm
        adapt = dot(norm, ada_w_ref[0])
        scale0[lo:hi] = sigmoid(adapt[:, :width] + ada_b_ref[0:1])
        shift0[lo:hi] = adapt[:, width:]

    def gates():
        def adapt_piece(lo, hi):
            adapt = dot(norm_ref[first + lo : first + hi], ada_w_ref[1])
            scale1[lo:hi] = sigmoid(adapt[:, :width] + ada_b_ref[1:2])
            shift1[lo:hi] = adapt[:, width:]

        def zero_piece(lo, hi):
            norm = norm_ref[first + lo : first + hi]
            gate0[lo:hi] = sigmoid(dot(norm, zero_w_ref[0]) + zero_b_ref[0:1])
            gate1[lo:hi] = sigmoid(dot(norm, zero_w_ref[1]) + zero_b_ref[1:2])

        def edge_piece(e):
            x = (left_ref, right_ref)[e]
            start = (samples + 1) * HALO
            x = x[start : start + EDGE_Q * 16]
            x = jnp.concatenate([x, jnp.zeros_like(x)], axis=0)
            got = pair_scale(*pair_sums(x, lhs_ref[...], heads))
            for h in range(heads):
                edge_bias[e, h * EDGE_Q : (h + 1) * EDGE_Q] = got[h * 16 : h * 16 + EDGE_Q]

        out = [lambda e=e: edge_piece(e) for e in range(2)]
        return out + skew(each(adapt_piece, rows, 4), each(zero_piece, rows, 4))

    def prepare(s):
        def norm_piece(lo, hi):
            x = stream_rows(s, lo, hi).astype(F32)
            y = norm_rows(x) * scale0[lo:hi] + shift0[lo:hi]
            attn_ref[s, lo:hi] = y.astype(BF16)

        def keyval_piece(lo, hi):
            y = dot(attn_ref[s, lo:hi], qkvg_ref[:, width : 3 * width])
            k_ref[s, lo:hi] = y[:, :width].astype(BF16)
            v_ref[s, lo:hi] = y[:, width:].astype(BF16)

        def query_piece(lo, hi):
            lo, hi = max(lo - first, 0), min(hi - first, rows)
            y = dot(attn_ref[s, first + lo : first + hi], wqg_ref[...])
            q_ref[s, lo:hi] = ((y[:, :width] + query_b_ref[0:1]) * factor).astype(BF16)
            gate_ref[s, lo:hi] = sigmoid(y[:, width:])

        stages = [each(f, ext, 4) for f in (norm_piece, keyval_piece, query_piece)]
        if s == 0:
            stages = [each(cond_piece, ext, 4)] + stages
        return skew(*stages)

    def attend(s):
        def score(t):
            r, n, key, w = places[t]
            if n >= 16:
                q = q_ref[s, r : r + n]
                wide = jnp.concatenate([q * masks[h] for h in range(heads)], axis=0)
                bias = bias_ref[w]
            else:
                base = r // 16 * 16
                q = q_ref[s, base : base + 16].astype(F32)[r - base : r - base + n]
                wide = jnp.concatenate(
                    [jnp.where(lane_head == h, q, 0.0) for h in range(heads)], axis=0
                ).astype(BF16)
                bias = edge_bias[0 if w < 0 else 1]
            got = dot_t(wide, k_ref[s, key : key + key_len])
            if 1 < w < windows - 2:
                got = got + bias
            else:
                got = got + (bias + live_ref[w + 1 : w + 2])
            score_ref[s % 2, t, : heads * n] = got

        def soften(t):
            n = heads * places[t][1]
            x = score_ref[s % 2, t, :n]
            weights = jnp.exp(x - jnp.max(x, -1, keepdims=True))
            prob_ref[s % 2, t, :n] = weights.astype(BF16)
            sums = jnp.sum(weights, -1, keepdims=True)
            n = places[t][1]
            pick = jnp.broadcast_to(sums[0:n], (n, width))
            for h in range(1, heads):
                pick = jnp.where(lane_head == h, sums[h * n : (h + 1) * n], pick)
            total_ref[s % 2, t, :n] = pick

        def blend(t):
            r, n, key, w = places[t]
            out = dot(prob_ref[s % 2, t, : heads * n], v_ref[s, key : key + key_len])
            pick = out[0:n]
            for h in range(1, heads):
                pick = jnp.where(lane_head == h, out[h * n : (h + 1) * n], pick)
            got = pick / total_ref[s % 2, t, :n] * gate_ref[s, r : r + n]
            if n < 16:
                pad = jnp.zeros_like(got)
                base = r // 16 * 16
                got = jnp.concatenate([pad, got] if r > base else [got, pad], axis=0)
                r, n = base, 16
            blend_ref[s, r : r + n] = got.astype(BF16)

        count = len(places)
        out = []
        for t in range(count + 4):
            if t < count:
                out.append(lambda t=t: score(t))
            if 0 <= t - 2 < count:
                out.append(lambda t=t: soften(t - 2))
            if 0 <= t - 4 < count:
                out.append(lambda t=t: blend(t - 4))
        return out

    def out_copies(s):
        return (
            pltpu.make_async_copy(
                result_ref.at[s, pl.ds(EDGE, atom_dev)], atoms_hbm.at[s], sems.at[0, s]
            ),
            pltpu.make_async_copy(tokens_ref.at[s], tokens_hbm.at[s], sems.at[1, s]),
        )

    def finish(s):
        def after_piece(lo, hi):
            x = stream_rows(s, first + lo, first + hi).astype(F32)
            y = (x + gate0[lo:hi] * dot(blend_ref[s, lo:hi], out_w_ref[...])).astype(BF16)
            after_ref[s, lo:hi] = y
            z = norm_rows(y.astype(F32)) * scale1[lo:hi] + shift1[lo:hi]
            trans_ref[s, lo:hi] = z.astype(BF16)

        def hidden_piece(lo, hi):
            y = dot(trans_ref[s, lo:hi], swiglu_ref[...])
            a = y[:, :hidden]
            hidden_ref[s, lo:hi] = (a * sigmoid(a) * y[:, hidden:]).astype(BF16)

        def result_piece(lo, hi):
            y = gate1[lo:hi] * dot(hidden_ref[s, lo:hi], down_ref[...])
            result_ref[s, lo:hi] = (after_ref[s, lo:hi].astype(F32) + y).astype(BF16)

        def feature_piece(lo, hi):
            y = dot(result_ref[s, lo:hi], token_w_ref[...])
            feature_ref[s % 2, lo:hi] = jnp.maximum(y, 0.0).astype(BF16)

        def token_piece(lo, hi):
            y = dot(onehot_ref[:, :rows], feature_ref[s % 2, :, lo:hi])
            for c in range(lo, hi, 128):
                z = y[:, c - lo : c - lo + 128] * inverse_ref[...]
                tokens_ref[s, :, c : c + 128] = z.astype(BF16)

        def send():
            for c in out_copies(s):
                c.start()

        stages = (after_piece, hidden_piece, result_piece, feature_piece)
        out = skew(*[each(f, rows, PIECES) for f in stages])
        out += [lambda lo=lo: token_piece(lo, lo + 256) for lo in range(0, token_width, 256)]
        return out + [send]

    weave(prepare(0))
    for s in range(samples):
        weave(
            attend(s),
            finish(s - 1) if s > 0 else gates(),
            prepare(s + 1) if s + 1 < samples else None,
        )
    weave(finish(samples - 1))
    for s in range(samples):
        for c in out_copies(s):
            c.wait()


def on_device(
    atoms_in,
    cond,
    pair,
    atom_mask,
    atom_count,
    atom_to_token,
    ada_weight,
    ada_bias,
    zero_weight,
    zero_bias,
    qkvg_weight,
    query_bias,
    pair_weight,
    out_weight,
    swiglu_weight,
    down_weight,
    token_weight,
):
    samples, atom_dev, width = atoms_in.shape
    windows, query_len, channels, key_len = pair.shape
    count_row = jnp.broadcast_to(atom_count, (8, 128))
    heads = pair_weight.shape[0]
    hidden = down_weight.shape[0]
    token_width = token_weight.shape[1]
    tok_dev = atom_dev // ATOMS_PER_TOKEN
    ext = atom_dev + 2 * HALO
    rows = atom_dev + 2 * EDGE
    far = pl.BlockSpec(memory_space=pltpu.HBM)
    vmem = pl.BlockSpec(memory_space=pltpu.VMEM)

    def near(array):
        return pltpu.with_memory_space_constraint(array, pltpu.VMEM)

    def away(array):
        return pltpu.with_memory_space_constraint(array, pltpu.HBM)

    wire_rows = (samples + 1) * HALO + EDGE_Q * channels + 16
    wire = pltpu.VMEM((wire_rows, width), BF16)
    pair = pair.reshape(windows, query_len * channels, key_len)
    across, within, info = pl.pallas_call(
        pack_kernel,
        out_shape=(wire, wire, pltpu.VMEM((16, atom_dev), F32)),
        in_specs=[far] * 5,
        out_specs=(vmem, vmem, vmem),
        scratch_shapes=[
            pltpu.VMEM((atom_dev,), jnp.int32),
            pltpu.VMEM((atom_dev,), jnp.int32),
            pltpu.SemaphoreType.DMA((2 * (samples + 3),)),
        ],
        compiler_params=pltpu.CompilerParams(vmem_limit_bytes=4 << 20),
        name="pack",
    )(*[away(a) for a in (atom_mask, atom_to_token, atoms_in, cond, pair)])
    count = lax.axis_size("atom")
    swaps = [[(i, i + 1) for i in range(at, count - 1, 2)] for at in (1, 0)]
    swaps = [pairs + [(j, i) for i, j in pairs] for pairs in swaps]
    across = lax.ppermute(across, "atom", swaps[0])
    within = lax.ppermute(within, "atom", swaps[1])

    lhs_shape = (3 * 16 * heads, 16 * channels)
    bias, lhs = pl.pallas_call(
        bias_kernel,
        out_shape=(
            pltpu.VMEM((windows, heads * query_len, key_len), F32),
            pltpu.VMEM(lhs_shape, BF16),
        ),
        in_specs=[vmem] * 4,
        out_specs=(vmem, vmem),
        scratch_shapes=[
            pltpu.VMEM((4, 16 * heads, key_len), F32),
            pltpu.VMEM((4, 2, 128, key_len), BF16),
            pltpu.VMEM((16, key_len), F32),
        ],
        compiler_params=pltpu.CompilerParams(vmem_limit_bytes=8 << 20),
        name="bias",
    )(near(count_row), pair_weight, near(info), near(pair))

    weights = (
        ada_weight,
        ada_bias,
        zero_weight,
        zero_bias,
        qkvg_weight,
        query_bias.reshape(1, width),
        out_weight,
        swiglu_weight,
        down_weight,
        token_weight,
    )
    operands = (atoms_in, count_row, info, cond, across, within, bias, lhs) + weights
    return pl.pallas_call(
        block_kernel,
        out_shape=(
            jax.ShapeDtypeStruct((samples, atom_dev, width), BF16),
            jax.ShapeDtypeStruct((samples, tok_dev, token_width), BF16),
        ),
        in_specs=[vmem] * len(operands),
        out_specs=(far, far),
        scratch_shapes=[
            pltpu.VMEM((ext, width), F32),
            pltpu.VMEM((ext, width), F32),
            pltpu.VMEM((rows, width), F32),
            pltpu.VMEM((rows, width), F32),
            pltpu.VMEM((rows, width), F32),
            pltpu.VMEM((rows, width), F32),
            pltpu.VMEM((2, heads * EDGE_Q, key_len), F32),
            pltpu.VMEM((16, key_len), F32),
            pltpu.VMEM((tok_dev, 512), BF16),
            pltpu.VMEM((tok_dev, 128), F32),
            pltpu.VMEM((wire_rows, width), BF16),
            pltpu.VMEM((wire_rows, width), BF16),
            pltpu.VMEM((ext, width), BF16),
            pltpu.VMEM((width, 2 * width), BF16),
            pltpu.VMEM((samples, ext, width), BF16),
            pltpu.VMEM((samples, rows, width), BF16),
            pltpu.VMEM((samples, ext, width), BF16),
            pltpu.VMEM((samples, ext, width), BF16),
            pltpu.VMEM((samples, rows, width), F32),
            pltpu.VMEM((2, windows + 2, heads * query_len, key_len), F32),
            pltpu.VMEM((2, windows + 2, heads * query_len, key_len), BF16),
            pltpu.VMEM((2, windows + 2, query_len, width), F32),
            pltpu.VMEM((samples, rows, width), BF16),
            pltpu.VMEM((samples, rows, width), BF16),
            pltpu.VMEM((samples, rows, width), BF16),
            pltpu.VMEM((samples, rows, hidden), BF16),
            pltpu.VMEM((samples, rows, width), BF16),
            pltpu.VMEM((2, rows, token_width), BF16),
            pltpu.VMEM((samples, tok_dev, token_width), BF16),
            pltpu.SemaphoreType.DMA((2, samples)),
        ],
        compiler_params=pltpu.CompilerParams(vmem_limit_bytes=24 << 20),
        name="block",
    )(*[near(a) for a in operands])


def solution(mesh):
    in_specs = (
        P("struct", "atom", None),
        P(("struct", "atom"), None),
        P(("struct", "atom"), None, None, None),
        P(("struct", "atom")),
        P("struct"),
        P(("struct", "atom")),
        P(),
        P(),
        P(),
        P(),
        P(),
        P(),
        P(),
        P(),
        P(),
        P(),
        P(),
    )
    out_specs = (P("struct", "atom", None), P("struct", "atom", None))
    return jax.shard_map(
        on_device, mesh=mesh, in_specs=in_specs, out_specs=out_specs, check_vma=False
    )
```

```python
import functools

import jax
import jax.numpy as jnp
from jax import lax
from jax.experimental import pallas as pl
from jax.experimental.pallas import tpu as pltpu
from jax.sharding import PartitionSpec as P

ATOMS_PER_TOKEN = 8
EPS = 1e-05
HALO = 80
EDGE = 16
EDGE_Q = 8
MASKED = -1e30
BF16 = jnp.bfloat16
F32 = jnp.float32


def dot(a, b):
    return jnp.dot(a, b, preferred_element_type=F32)


def dot_t(a, b):
    return lax.dot_general(a, b, (((1,), (1,)), ((), ())), preferred_element_type=F32)


def norm_rows(x):
    center = jnp.mean(x, -1, keepdims=True)
    off = x - center
    spread = jnp.mean(jnp.square(off), -1, keepdims=True)
    return off * lax.rsqrt(spread + EPS)


def sigmoid(x):
    return 0.5 * jnp.tanh(0.5 * x) + 0.5


def iota(shape, dim):
    return lax.broadcasted_iota(jnp.int32, shape, dim)


def pack_kernel(
    mask_hbm,
    token_hbm,
    atoms_ref,
    cond_ref,
    pair_ref,
    ada_hbm,
    zero_hbm,
    qkvg_hbm,
    across_ref,
    within_ref,
    info_ref,
    ada_ref,
    zero_ref,
    qkvg_ref,
    mask_ref,
    token_ref,
    sems,
):
    samples, atom_dev, _ = atoms_ref.shape
    windows, pair_rows, _ = pair_ref.shape
    edge_rows = EDGE_Q * 16
    copies = []

    def copy(src, dst):
        c = pltpu.make_async_copy(src, dst, sems.at[len(copies)])
        c.start()
        copies.append(c)

    copy(mask_hbm, mask_ref)
    copy(token_hbm, token_ref)
    rows = (samples + 1) * HALO
    device = lax.axis_index("atom")
    odd = device % 2
    for wire, last in ((across_ref, odd), (within_ref, 1 - odd)):
        at = pl.multiple_of(last * (atom_dev - HALO), 16)
        w = last * (windows - 1)
        p = pl.multiple_of(last * (pair_rows - edge_rows), 16)
        for s in range(samples):
            copy(atoms_ref.at[s, pl.ds(at, HALO)], wire.at[pl.ds(s * HALO, HALO)])
        copy(cond_ref.at[pl.ds(at, HALO)], wire.at[pl.ds(samples * HALO, HALO)])
        copy(pair_ref.at[w, pl.ds(p, edge_rows)], wire.at[pl.ds(rows, edge_rows)])
    rows += edge_rows
    for c in copies[:2]:
        c.wait()
    for src, dst in ((ada_hbm, ada_ref), (zero_hbm, zero_ref), (qkvg_hbm, qkvg_ref)):
        copy(src, dst)
    mask = mask_ref[...].reshape(1, atom_dev)
    token = token_ref[...].reshape(1, atom_dev)
    exists = jnp.where(mask == 1, 1.0, 0.0)
    own = (token - device * (atom_dev // ATOMS_PER_TOKEN)).astype(F32)
    row = iota((16, atom_dev), 0)
    info = jnp.where(row == 0, exists, jnp.where(row == 1, own, 0.0))
    info_ref[...] = info
    end = info[:, atom_dev - 128 :]
    start = info[:, :128]
    across_ref[rows : rows + 16] = jnp.where(odd == 1, end, start).astype(BF16)
    within_ref[rows : rows + 16] = jnp.where(odd == 1, start, end).astype(BF16)
    for c in copies[2:]:
        c.wait()


def pair_lhs(weight_ref, lhs_ref):
    heads, channels = weight_ref.shape
    wide = 16 * channels
    w = weight_ref[...]
    w = w - jnp.mean(w, -1, keepdims=True)
    spread = jnp.where(iota((channels, wide), 1) % channels == iota((channels, wide), 0), 1.0, 0.0)
    tiled = jnp.dot(w, spread, precision=lax.Precision.HIGHEST, preferred_element_type=F32)
    full = jnp.concatenate(
        [jnp.broadcast_to(tiled[h : h + 1], (16, wide)) for h in range(heads)], axis=0
    )
    shape = (16 * heads, wide)
    full = jnp.where(iota(shape, 1) // channels == iota(shape, 0) % 16, full, 0.0)
    high = full.astype(BF16)
    rest = full - high.astype(F32)
    mid = rest.astype(BF16)
    low = (rest - mid.astype(F32)).astype(BF16)
    n = 16 * heads
    lhs_ref[0:n] = high
    lhs_ref[n : 2 * n] = mid
    lhs_ref[2 * n : 3 * n] = low


def pair_sums(x, lhs, heads):
    n = 16 * heads
    out = dot(lhs, x)
    rows = x.astype(F32).reshape(16, 16, -1)
    off = rows - jnp.mean(rows, axis=1, keepdims=True)
    square = off * off
    half = (square[:, :8] + square[:, 8:]).reshape(128, -1)
    high = half.astype(BF16)
    low = (half - high.astype(F32)).astype(BF16)
    sums = out[0:n] + out[n : 2 * n] + out[2 * n : 3 * n]
    return sums, high, low


def pair_scale(sums, high, low):
    gather = jnp.where(iota((16, 128), 1) // 8 == iota((16, 128), 0), 1.0 / 16, 0.0).astype(BF16)
    rstd = lax.rsqrt(dot(gather, high) + dot(gather, low) + EPS)
    return sums * jnp.concatenate([rstd] * (sums.shape[0] // 16), axis=0)


def usable_only(flags, start, atom_dev, count_ref):
    lanes = flags.shape[1]
    device = lax.axis_index("atom")
    position = device * atom_dev + start + iota((1, lanes), 1)
    count = jnp.broadcast_to(count_ref[0:1, 0:1], (1, lanes))
    return jnp.where(position < count, flags, 0.0)


def live_rows(flags, wanted, query_len, key_len, live_ref):
    total = flags.shape[1]
    flags8 = jnp.broadcast_to(flags, (8, total))
    rolled = {}
    for n, w in wanted:
        start = 128 + query_len * w - (key_len - query_len) // 2
        shift = start % 128
        if shift not in rolled:
            rolled[shift] = pltpu.roll(flags8, total - shift, 1)
        row = rolled[shift][0:1, start - shift : start - shift + key_len]
        live_ref[n : n + 1] = jnp.where(row > 0.5, 0.0, MASKED)


def early_kernel(
    count_ref,
    weight_ref,
    info_ref,
    pair_ref,
    cond_ref,
    atoms_ref,
    ada_w_ref,
    ada_b_ref,
    zero_w_ref,
    zero_b_ref,
    qkvg_ref,
    query_b_ref,
    bias_ref,
    lhs_ref,
    scale0,
    shift0,
    scale1,
    shift1,
    gate0,
    gate1,
    k_ref,
    v_ref,
    q_ref,
    gate_ref,
    wqg_ref,
    sum_ref,
    half_ref,
    live_ref,
    norm_ref,
    attn_ref,
):
    heads = weight_ref.shape[0]
    windows, score_rows, key_len = bias_ref.shape
    query_len = score_rows // heads
    pair_lhs(weight_ref, lhs_ref)
    ones = jnp.ones((1, 128), F32)
    flags = jnp.concatenate([ones, usable_only(info_ref[0:1], 0, info_ref.shape[1], count_ref), ones], axis=1)
    live_rows(flags, [(w, w) for w in range(windows)], query_len, key_len, live_ref)
    per = query_len // 16
    n = 16 * heads

    def first(c):
        x = pair_ref[c // per, c % per * 256 : c % per * 256 + 256]
        sum_ref[c % 4], half_ref[c % 4, 0], half_ref[c % 4, 1] = pair_sums(
            x, lhs_ref[...], heads
        )

    def second(c):
        got = pair_scale(sum_ref[c % 4], half_ref[c % 4, 0], half_ref[c % 4, 1])
        w = c // per
        live = live_ref[w : w + 1]
        for h in range(heads):
            at = h * query_len + c % per * 16
            bias_ref[w, at : at + 16] = got[h * 16 : h * 16 + 16] + live

    atom_dev, width = cond_ref.shape
    factor = (width // heads) ** (-0.5)
    wqg_ref[:, :width] = qkvg_ref[:, :width]
    wqg_ref[:, width:] = qkvg_ref[:, 3 * width :]

    def cond_piece(lo, hi):
        norm_ref[lo:hi], scale0[lo:hi], shift0[lo:hi] = cond_rows(
            cond_ref[lo:hi], ada_w_ref, ada_b_ref
        )

    def adapt_piece(lo, hi):
        scale1[lo:hi], shift1[lo:hi] = adapt_rows(norm_ref[lo:hi], ada_w_ref, ada_b_ref)

    def zero_piece(lo, hi):
        gate0[lo:hi], gate1[lo:hi] = zero_rows(norm_ref[lo:hi], zero_w_ref, zero_b_ref)

    def attn_piece(lo, hi):
        attn_ref[lo:hi] = attn_rows(atoms_ref[0, lo:hi], scale0[lo:hi], shift0[lo:hi])

    def keyval_piece(lo, hi):
        k_ref[lo:hi], v_ref[lo:hi] = keyval_rows(attn_ref[lo:hi], qkvg_ref)

    def query_piece(lo, hi):
        q_ref[lo:hi], gate_ref[lo:hi] = query_rows(
            attn_ref[lo:hi], wqg_ref, query_b_ref, factor
        )

    own = (cond_piece, adapt_piece, zero_piece, attn_piece, keyval_piece, query_piece)
    chunks = range(windows * per)
    weave(
        skew([lambda c=c: first(c) for c in chunks], [lambda c=c: second(c) for c in chunks]),
        skew(*[each(f, atom_dev, 3) for f in own]),
    )


def cond_rows(x, ada_w_ref, ada_b_ref):
    norm = norm_rows(x.astype(F32)).astype(BF16)
    adapt = dot(norm, ada_w_ref[0])
    width = norm.shape[1]
    return norm, sigmoid(adapt[:, :width] + ada_b_ref[0:1]), adapt[:, width:]


def adapt_rows(norm, ada_w_ref, ada_b_ref):
    adapt = dot(norm, ada_w_ref[1])
    width = norm.shape[1]
    return sigmoid(adapt[:, :width] + ada_b_ref[1:2]), adapt[:, width:]


def zero_rows(norm, zero_w_ref, zero_b_ref):
    return [sigmoid(dot(norm, zero_w_ref[u]) + zero_b_ref[u : u + 1]) for u in range(2)]


def attn_rows(x, scale, shift):
    return (norm_rows(x.astype(F32)) * scale + shift).astype(BF16)


def keyval_rows(attn, qkvg_ref):
    width = attn.shape[1]
    y = dot(attn, qkvg_ref[:, width : 3 * width]).astype(BF16)
    return y[:, :width], y[:, width:]


def query_rows(attn, wqg_ref, query_b_ref, factor):
    width = attn.shape[1]
    y = dot(attn, wqg_ref[...])
    return ((y[:, :width] + query_b_ref[0:1]) * factor).astype(BF16), sigmoid(y[:, width:])


def each(step, n, pieces):
    size = -(-n // pieces // 16) * 16
    return [lambda lo=lo, hi=min(n, lo + size): step(lo, hi) for lo in range(0, n, size)]


PIECES = 4


def weave(*streams):
    steps = [x for x in streams if x]
    total = max(len(x) for x in steps)
    done = [0] * len(steps)
    for t in range(total):
        for n, x in enumerate(steps):
            while done[n] * total < (t + 1) * len(x) and done[n] < len(x):
                x[done[n]]()
                done[n] += 1


def skew(*stages):
    pieces = len(stages[0])
    out = []
    for t in range(pieces + len(stages) - 1):
        for n, stage in enumerate(stages):
            if 0 <= t - n < pieces:
                out.append(stage[t - n])
    return out


def block_kernel(
    atoms_ref,
    count_ref,
    info_ref,
    across_ref,
    within_ref,
    bias_ref,
    lhs_ref,
    scale0_own,
    shift0_own,
    scale1_own,
    shift1_own,
    gate0_own,
    gate1_own,
    k_own,
    v_own,
    q_own,
    gate_own,
    wqg_ref,
    ada_w_ref,
    ada_b_ref,
    zero_w_ref,
    zero_b_ref,
    qkvg_ref,
    query_b_ref,
    out_w_ref,
    swiglu_ref,
    down_ref,
    token_w_ref,
    atoms_hbm,
    tokens_hbm,
    scale0,
    shift0,
    scale1,
    shift1,
    gate0,
    gate1,
    edge_bias,
    live_ref,
    onehot_ref,
    inverse_ref,
    left_ref,
    right_ref,
    attn_ref,
    q_ref,
    k_ref,
    v_ref,
    gate_ref,
    score_ref,
    prob_ref,
    total_ref,
    blend_ref,
    after_ref,
    trans_ref,
    hidden_ref,
    result_ref,
    feature_ref,
    tokens_ref,
    sems,
):
    samples, atom_dev, width = atoms_ref.shape
    windows, score_rows, key_len = bias_ref.shape
    query_len = atom_dev // windows
    heads = score_rows // query_len
    head_dim = width // heads
    margin = (key_len - query_len) // 2
    tok_dev = atom_dev // ATOMS_PER_TOKEN
    ext = atom_dev + 2 * HALO
    rows = atom_dev + 2 * EDGE
    first = HALO - EDGE
    hidden = down_ref.shape[0]
    token_width = token_w_ref.shape[1]
    factor = head_dim ** (-0.5)

    odd = lax.axis_index("atom") % 2 == 1
    left_ref[...] = jnp.where(odd, within_ref[...], across_ref[...])
    right_ref[...] = jnp.where(odd, across_ref[...], within_ref[...])
    at = samples * HALO
    at += HALO + EDGE_Q * 16
    exists = info_ref[0:1]
    own = info_ref[1:2]
    info_l = left_ref[at : at + 16].astype(F32)
    info_r = right_ref[at : at + 16].astype(F32)
    flags = jnp.concatenate([info_l[0:1], exists, info_r[0:1]], axis=1)
    flags = usable_only(flags, -128, atom_dev, count_ref)
    tokens = jnp.concatenate([info_l[1:2] - tok_dev, own, info_r[1:2] + tok_dev], axis=1)
    total = flags.shape[1]
    lane = iota((1, total), 1)
    halo = jnp.where((lane >= 128) & (lane < 128 + atom_dev), 1.0, flags)
    inner = [(w + 1, w) for w in (0, 1, windows - 2, windows - 1)]
    live_rows(halo, inner, query_len, key_len, live_ref)
    outer = [(w + 1, w) for w in (-1, windows)]
    live_rows(flags, outer, query_len, key_len, live_ref)
    flags8 = jnp.broadcast_to(flags, (8, total))
    shift = 128 - EDGE
    flags = pltpu.roll(flags8, total - shift, 1)[0:1]
    tokens = pltpu.roll(jnp.broadcast_to(tokens, (8, total)), total - shift, 1)[0:1]
    lanes = onehot_ref.shape[1]
    slot = iota((tok_dev, lanes), 0).astype(F32)
    inside = iota((tok_dev, lanes), 1) < rows
    hit = (tokens[:, :lanes] == slot) & (flags[:, :lanes] > 0.5) & inside
    onehot = jnp.where(hit, 1.0, 0.0)
    onehot_ref[...] = onehot.astype(BF16)
    counts = jnp.sum(onehot, -1, keepdims=True)
    inverse_ref[...] = jnp.broadcast_to(1.0 / jnp.maximum(counts, 1.0), inverse_ref.shape)

    lane_head = iota((1, width), 1) // head_dim
    masks = [jnp.where(lane_head == h, 1.0, 0.0).astype(BF16) for h in range(heads)]
    places = [
        (EDGE + w * query_len, query_len, HALO + w * query_len - margin, w)
        for w in range(windows)
    ]
    for w, r in ((-1, EDGE - EDGE_Q), (windows, EDGE + atom_dev)):
        places.append((r, EDGE_Q, HALO + w * query_len - margin, w))

    def spliced(middle, off, lo, hi):
        parts = []
        for base, size, ref, start in (
            (0, HALO, left_ref, off),
            (HALO, atom_dev, middle, 0),
            (HALO + atom_dev, HALO, right_ref, off),
        ):
            x, y = max(lo, base), min(hi, base + size)
            if x < y:
                parts.append(ref[x - base + start : y - base + start])
        return parts[0] if len(parts) == 1 else jnp.concatenate(parts, axis=0)

    def stream_rows(s, lo, hi):
        return spliced(atoms_ref.at[s], s * HALO, lo, hi)

    def join(own, halo, lo, hi):
        side = halo.shape[0] // 2
        parts = []
        for base, size, ref, start in (
            (0, side, halo, 0),
            (side, atom_dev, own, 0),
            (side + atom_dev, side, halo, side),
        ):
            x, y = max(lo, base), min(hi, base + size)
            if x < y:
                parts.append(ref[x - base + start : y - base + start])
        return parts[0] if len(parts) == 1 else jnp.concatenate(parts, axis=0)

    def halos(off):
        return jnp.concatenate([left_ref[off : off + HALO], right_ref[off : off + HALO]], axis=0)

    def lead():
        def cond_step():
            norm, scale0[...], shift0[...] = cond_rows(
                halos(samples * HALO), ada_w_ref, ada_b_ref
            )
            norm = norm[first : first + 2 * EDGE]
            scale1[...], shift1[...] = adapt_rows(norm, ada_w_ref, ada_b_ref)
            gate0[...], gate1[...] = zero_rows(norm, zero_w_ref, zero_b_ref)

        def attn_step():
            attn = attn_rows(halos(0), scale0[...], shift0[...])
            k, v = keyval_rows(attn, qkvg_ref)
            end = HALO + atom_dev
            k_ref[0, :HALO], k_ref[0, end:] = k[:HALO], k[HALO:]
            v_ref[0, :HALO], v_ref[0, end:] = v[:HALO], v[HALO:]
            q, gate = query_rows(attn[first : first + 2 * EDGE], wqg_ref, query_b_ref, factor)
            end = EDGE + atom_dev
            q_ref[0, :EDGE], q_ref[0, end:] = q[:EDGE], q[EDGE:]
            gate_ref[0, :EDGE], gate_ref[0, end:] = gate[:EDGE], gate[EDGE:]

        def copy_step():
            k_ref[0, HALO : HALO + atom_dev] = k_own[...]
            v_ref[0, HALO : HALO + atom_dev] = v_own[...]
            q_ref[0, EDGE : EDGE + atom_dev] = q_own[...]
            gate_ref[0, EDGE : EDGE + atom_dev] = gate_own[...]

        def edge_step(e):
            x = (left_ref, right_ref)[e]
            start = (samples + 1) * HALO
            x = x[start : start + EDGE_Q * 16]
            x = jnp.concatenate([x, jnp.zeros_like(x)], axis=0)
            got = pair_scale(*pair_sums(x, lhs_ref[...], heads))
            for h in range(heads):
                edge_bias[e, h * EDGE_Q : (h + 1) * EDGE_Q] = got[h * 16 : h * 16 + EDGE_Q]

        return [copy_step, cond_step, attn_step] + [lambda e=e: edge_step(e) for e in range(2)]

    def prepare(s):
        def norm_piece(lo, hi):
            attn_ref[s, lo:hi] = attn_rows(
                stream_rows(s, lo, hi),
                join(scale0_own, scale0, lo, hi),
                join(shift0_own, shift0, lo, hi),
            )

        def keyval_piece(lo, hi):
            k_ref[s, lo:hi], v_ref[s, lo:hi] = keyval_rows(attn_ref[s, lo:hi], qkvg_ref)

        def query_piece(lo, hi):
            lo, hi = max(lo - first, 0), min(hi - first, rows)
            q_ref[s, lo:hi], gate_ref[s, lo:hi] = query_rows(
                attn_ref[s, first + lo : first + hi], wqg_ref, query_b_ref, factor
            )

        return skew(*[each(f, ext, 4) for f in (norm_piece, keyval_piece, query_piece)])

    def attend(s):
        def score(t):
            r, n, key, w = places[t]
            if n >= 16:
                q = q_ref[s, r : r + n]
                wide = jnp.concatenate([q * masks[h] for h in range(heads)], axis=0)
                bias = bias_ref[w]
            else:
                base = r // 16 * 16
                q = q_ref[s, base : base + 16].astype(F32)[r - base : r - base + n]
                wide = jnp.concatenate(
                    [jnp.where(lane_head == h, q, 0.0) for h in range(heads)], axis=0
                ).astype(BF16)
                bias = edge_bias[0 if w < 0 else 1]
            got = dot_t(wide, k_ref[s, key : key + key_len])
            if 1 < w < windows - 2:
                got = got + bias
            else:
                got = got + (bias + live_ref[w + 1 : w + 2])
            score_ref[s % 2, t, : heads * n] = got

        def soften(t):
            n = heads * places[t][1]
            x = score_ref[s % 2, t, :n]
            weights = jnp.exp(x - jnp.max(x, -1, keepdims=True))
            prob_ref[s % 2, t, :n] = weights.astype(BF16)
            sums = jnp.sum(weights, -1, keepdims=True)
            n = places[t][1]
            pick = jnp.broadcast_to(sums[0:n], (n, width))
            for h in range(1, heads):
                pick = jnp.where(lane_head == h, sums[h * n : (h + 1) * n], pick)
            total_ref[s % 2, t, :n] = pick

        def blend(t):
            r, n, key, w = places[t]
            out = dot(prob_ref[s % 2, t, : heads * n], v_ref[s, key : key + key_len])
            pick = out[0:n]
            for h in range(1, heads):
                pick = jnp.where(lane_head == h, out[h * n : (h + 1) * n], pick)
            got = pick / total_ref[s % 2, t, :n] * gate_ref[s, r : r + n]
            if n < 16:
                pad = jnp.zeros_like(got)
                base = r // 16 * 16
                got = jnp.concatenate([pad, got] if r > base else [got, pad], axis=0)
                r, n = base, 16
            blend_ref[s, r : r + n] = got.astype(BF16)

        count = len(places)
        out = []
        for t in range(count + 4):
            if t < count:
                out.append(lambda t=t: score(t))
            if 0 <= t - 2 < count:
                out.append(lambda t=t: soften(t - 2))
            if 0 <= t - 4 < count:
                out.append(lambda t=t: blend(t - 4))
        return out

    def out_copies(s):
        return (
            pltpu.make_async_copy(
                result_ref.at[s, pl.ds(EDGE, atom_dev)], atoms_hbm.at[s], sems.at[0, s]
            ),
            pltpu.make_async_copy(tokens_ref.at[s], tokens_hbm.at[s], sems.at[1, s]),
        )

    def finish(s):
        def after_piece(lo, hi):
            x = stream_rows(s, first + lo, first + hi).astype(F32)
            y = (x + join(gate0_own, gate0, lo, hi) * dot(blend_ref[s, lo:hi], out_w_ref[...])).astype(BF16)
            after_ref[s, lo:hi] = y
            trans_ref[s, lo:hi] = attn_rows(
                y, join(scale1_own, scale1, lo, hi), join(shift1_own, shift1, lo, hi)
            )

        def hidden_piece(lo, hi):
            y = dot(trans_ref[s, lo:hi], swiglu_ref[...])
            a = y[:, :hidden]
            hidden_ref[s, lo:hi] = (a * sigmoid(a) * y[:, hidden:]).astype(BF16)

        def result_piece(lo, hi):
            y = join(gate1_own, gate1, lo, hi) * dot(hidden_ref[s, lo:hi], down_ref[...])
            result_ref[s, lo:hi] = (after_ref[s, lo:hi].astype(F32) + y).astype(BF16)

        def feature_piece(lo, hi):
            y = dot(result_ref[s, lo:hi], token_w_ref[...])
            feature_ref[s % 2, lo:hi] = jnp.maximum(y, 0.0).astype(BF16)

        def token_piece(lo, hi):
            y = dot(onehot_ref[:, :rows], feature_ref[s % 2, :, lo:hi])
            for c in range(lo, hi, 128):
                z = y[:, c - lo : c - lo + 128] * inverse_ref[...]
                tokens_ref[s, :, c : c + 128] = z.astype(BF16)

        def send():
            for c in out_copies(s):
                c.start()

        stages = (after_piece, hidden_piece, result_piece, feature_piece)
        out = skew(*[each(f, rows, PIECES) for f in stages])
        out += [lambda lo=lo: token_piece(lo, lo + 256) for lo in range(0, token_width, 256)]
        return out + [send]

    weave(lead())
    for s in range(samples):
        weave(
            attend(s),
            finish(s - 1) if s > 0 else None,
            prepare(s + 1) if s + 1 < samples else None,
        )
    weave(finish(samples - 1))
    for s in range(samples):
        for c in out_copies(s):
            c.wait()


def on_device(
    atoms_in,
    cond,
    pair,
    atom_mask,
    atom_count,
    atom_to_token,
    ada_weight,
    ada_bias,
    zero_weight,
    zero_bias,
    qkvg_weight,
    query_bias,
    pair_weight,
    out_weight,
    swiglu_weight,
    down_weight,
    token_weight,
):
    samples, atom_dev, width = atoms_in.shape
    windows, query_len, channels, key_len = pair.shape
    count_row = jnp.broadcast_to(atom_count, (8, 128))
    heads = pair_weight.shape[0]
    hidden = down_weight.shape[0]
    token_width = token_weight.shape[1]
    tok_dev = atom_dev // ATOMS_PER_TOKEN
    ext = atom_dev + 2 * HALO
    rows = atom_dev + 2 * EDGE
    far = pl.BlockSpec(memory_space=pltpu.HBM)
    vmem = pl.BlockSpec(memory_space=pltpu.VMEM)

    def near(array):
        return pltpu.with_memory_space_constraint(array, pltpu.VMEM)

    def away(array):
        return pltpu.with_memory_space_constraint(array, pltpu.HBM)

    wire_rows = (samples + 1) * HALO + EDGE_Q * channels + 16
    wire = pltpu.VMEM((wire_rows, width), BF16)
    early_weights = (ada_weight, zero_weight, qkvg_weight)
    pair = pair.reshape(windows, query_len * channels, key_len)
    across, within, info, ada_near, zero_near, qkvg_near = pl.pallas_call(
        pack_kernel,
        out_shape=(wire, wire, pltpu.VMEM((16, atom_dev), F32))
        + tuple(pltpu.VMEM(a.shape, a.dtype) for a in early_weights),
        in_specs=[far] * 8,
        out_specs=(vmem,) * 6,
        scratch_shapes=[
            pltpu.VMEM((atom_dev,), jnp.int32),
            pltpu.VMEM((atom_dev,), jnp.int32),
            pltpu.SemaphoreType.DMA((2 * samples + 9,)),
        ],
        compiler_params=pltpu.CompilerParams(vmem_limit_bytes=4 << 20),
        name="pack",
    )(*[away(a) for a in (atom_mask, atom_to_token, atoms_in, cond, pair) + early_weights])
    count = lax.axis_size("atom")
    swaps = [[(i, i + 1) for i in range(at, count - 1, 2)] for at in (1, 0)]
    swaps = [pairs + [(j, i) for i, j in pairs] for pairs in swaps]
    across = lax.ppermute(across, "atom", swaps[0])
    within = lax.ppermute(within, "atom", swaps[1])

    lhs_shape = (3 * 16 * heads, 16 * channels)
    shared = [
        near(a)
        for a in (
            atoms_in,
            ada_near,
            ada_bias,
            zero_near,
            zero_bias,
            qkvg_near,
            query_bias.reshape(1, width),
        )
    ]
    near_atoms, first_weights = shared[0], tuple(shared[1:])
    near_count = near(count_row)
    own_rows = pltpu.VMEM((atom_dev, width), F32)
    own_half = pltpu.VMEM((atom_dev, width), BF16)
    early = pl.pallas_call(
        early_kernel,
        out_shape=(
            pltpu.VMEM((windows, heads * query_len, key_len), F32),
            pltpu.VMEM(lhs_shape, BF16),
        )
        + (own_rows,) * 6
        + (own_half,) * 3
        + (own_rows, pltpu.VMEM((width, 2 * width), BF16)),
        in_specs=[vmem] * 12,
        out_specs=(vmem,) * 13,
        scratch_shapes=[
            pltpu.VMEM((4, 16 * heads, key_len), F32),
            pltpu.VMEM((4, 2, 128, key_len), BF16),
            pltpu.VMEM((16, key_len), F32),
            pltpu.VMEM((atom_dev, width), BF16),
            pltpu.VMEM((atom_dev, width), BF16),
        ],
        compiler_params=pltpu.CompilerParams(
            vmem_limit_bytes=8 << 20
        ),
        name="early",
    )(
        near_count, near(pair_weight), near(info), near(pair), near(cond), near_atoms, *first_weights
    )

    last_weights = [near(a) for a in (out_weight, swiglu_weight, down_weight, token_weight)]
    operands = (near_atoms, near_count, info, across, within) + tuple(early)
    operands = [near(a) if a is info else a for a in operands]
    operands += [*first_weights, *last_weights]
    return pl.pallas_call(
        block_kernel,
        out_shape=(
            jax.ShapeDtypeStruct((samples, atom_dev, width), BF16),
            jax.ShapeDtypeStruct((samples, tok_dev, token_width), BF16),
        ),
        in_specs=[vmem] * len(operands),
        out_specs=(far, far),
        scratch_shapes=[
            pltpu.VMEM((2 * HALO, width), F32),
            pltpu.VMEM((2 * HALO, width), F32),
            pltpu.VMEM((2 * EDGE, width), F32),
            pltpu.VMEM((2 * EDGE, width), F32),
            pltpu.VMEM((2 * EDGE, width), F32),
            pltpu.VMEM((2 * EDGE, width), F32),
            pltpu.VMEM((2, heads * EDGE_Q, key_len), F32),
            pltpu.VMEM((16, key_len), F32),
            pltpu.VMEM((tok_dev, 512), BF16),
            pltpu.VMEM((tok_dev, 128), F32),
            pltpu.VMEM((wire_rows, width), BF16),
            pltpu.VMEM((wire_rows, width), BF16),
            pltpu.VMEM((samples, ext, width), BF16),
            pltpu.VMEM((samples, rows, width), BF16),
            pltpu.VMEM((samples, ext, width), BF16),
            pltpu.VMEM((samples, ext, width), BF16),
            pltpu.VMEM((samples, rows, width), F32),
            pltpu.VMEM((2, windows + 2, heads * query_len, key_len), F32),
            pltpu.VMEM((2, windows + 2, heads * query_len, key_len), BF16),
            pltpu.VMEM((2, windows + 2, query_len, width), F32),
            pltpu.VMEM((samples, rows, width), BF16),
            pltpu.VMEM((samples, rows, width), BF16),
            pltpu.VMEM((samples, rows, width), BF16),
            pltpu.VMEM((samples, rows, hidden), BF16),
            pltpu.VMEM((samples, rows, width), BF16),
            pltpu.VMEM((2, rows, token_width), BF16),
            pltpu.VMEM((samples, tok_dev, token_width), BF16),
            pltpu.SemaphoreType.DMA((2, samples)),
        ],
        compiler_params=pltpu.CompilerParams(vmem_limit_bytes=24 << 20),
        name="block",
    )(*operands)


def solution(mesh):
    in_specs = (
        P("struct", "atom", None),
        P(("struct", "atom"), None),
        P(("struct", "atom"), None, None, None),
        P(("struct", "atom")),
        P("struct"),
        P(("struct", "atom")),
        P(),
        P(),
        P(),
        P(),
        P(),
        P(),
        P(),
        P(),
        P(),
        P(),
        P(),
    )
    out_specs = (P("struct", "atom", None), P("struct", "atom", None))
    return jax.shard_map(
        on_device, mesh=mesh, in_specs=in_specs, out_specs=out_specs, check_vma=False
    )
```

```python
import functools

import jax
import jax.numpy as jnp
from jax import lax
from jax.experimental import pallas as pl
from jax.experimental.pallas import tpu as pltpu
from jax.sharding import PartitionSpec as P

ATOMS_PER_TOKEN = 8
EPS = 1e-05
HALO = 80
EDGE = 16
EDGE_Q = 8
MASKED = -1e30
BF16 = jnp.bfloat16
F32 = jnp.float32


def dot(a, b):
    return jnp.dot(a, b, preferred_element_type=F32)


def dot_t(a, b):
    return lax.dot_general(a, b, (((1,), (1,)), ((), ())), preferred_element_type=F32)


def norm_rows(x):
    center = jnp.mean(x, -1, keepdims=True)
    off = x - center
    spread = jnp.mean(jnp.square(off), -1, keepdims=True)
    return off * lax.rsqrt(spread + EPS)


def sigmoid(x):
    return 0.5 * jnp.tanh(0.5 * x) + 0.5


def iota(shape, dim):
    return lax.broadcasted_iota(jnp.int32, shape, dim)


def pack_kernel(
    mask_hbm,
    token_hbm,
    atoms_ref,
    cond_ref,
    pair_ref,
    across_ref,
    within_ref,
    info_ref,
    mask_ref,
    token_ref,
    sems,
):
    samples, atom_dev, _ = atoms_ref.shape
    windows, pair_rows, _ = pair_ref.shape
    edge_rows = EDGE_Q * 16
    copies = []

    def copy(src, dst):
        c = pltpu.make_async_copy(src, dst, sems.at[len(copies)])
        c.start()
        copies.append(c)

    copy(mask_hbm, mask_ref)
    copy(token_hbm, token_ref)
    rows = (samples + 1) * HALO
    device = lax.axis_index("atom")
    odd = device % 2
    for wire, last in ((across_ref, odd), (within_ref, 1 - odd)):
        at = pl.multiple_of(last * (atom_dev - HALO), 16)
        w = last * (windows - 1)
        p = pl.multiple_of(last * (pair_rows - edge_rows), 16)
        for s in range(samples):
            copy(atoms_ref.at[s, pl.ds(at, HALO)], wire.at[pl.ds(s * HALO, HALO)])
        copy(cond_ref.at[pl.ds(at, HALO)], wire.at[pl.ds(samples * HALO, HALO)])
        copy(pair_ref.at[w, pl.ds(p, edge_rows)], wire.at[pl.ds(rows, edge_rows)])
    rows += edge_rows
    for c in copies[:2]:
        c.wait()
    mask = mask_ref[...].reshape(1, atom_dev)
    token = token_ref[...].reshape(1, atom_dev)
    exists = jnp.where(mask == 1, 1.0, 0.0)
    own = (token - device * (atom_dev // ATOMS_PER_TOKEN)).astype(F32)
    row = iota((16, atom_dev), 0)
    info = jnp.where(row == 0, exists, jnp.where(row == 1, own, 0.0))
    info_ref[...] = info
    end = info[:, atom_dev - 128 :]
    start = info[:, :128]
    across_ref[rows : rows + 16] = jnp.where(odd == 1, end, start).astype(BF16)
    within_ref[rows : rows + 16] = jnp.where(odd == 1, start, end).astype(BF16)
    for c in copies[2:]:
        c.wait()


def pair_lhs(weight_ref, lhs_ref):
    heads, channels = weight_ref.shape
    wide = 16 * channels
    w = weight_ref[...]
    w = w - jnp.mean(w, -1, keepdims=True)
    spread = jnp.where(iota((channels, wide), 1) % channels == iota((channels, wide), 0), 1.0, 0.0)
    tiled = jnp.dot(w, spread, precision=lax.Precision.HIGHEST, preferred_element_type=F32)
    full = jnp.concatenate(
        [jnp.broadcast_to(tiled[h : h + 1], (16, wide)) for h in range(heads)], axis=0
    )
    shape = (16 * heads, wide)
    full = jnp.where(iota(shape, 1) // channels == iota(shape, 0) % 16, full, 0.0)
    high = full.astype(BF16)
    rest = full - high.astype(F32)
    mid = rest.astype(BF16)
    low = (rest - mid.astype(F32)).astype(BF16)
    n = 16 * heads
    lhs_ref[0:n] = high
    lhs_ref[n : 2 * n] = mid
    lhs_ref[2 * n : 3 * n] = low


def pair_sums(x, lhs, heads):
    n = 16 * heads
    out = dot(lhs, x)
    rows = x.astype(F32).reshape(16, 16, -1)
    off = rows - jnp.mean(rows, axis=1, keepdims=True)
    square = off * off
    half = (square[:, :8] + square[:, 8:]).reshape(128, -1)
    high = half.astype(BF16)
    low = (half - high.astype(F32)).astype(BF16)
    sums = out[0:n] + out[n : 2 * n] + out[2 * n : 3 * n]
    return sums, high, low


def pair_scale(sums, high, low):
    gather = jnp.where(iota((16, 128), 1) // 8 == iota((16, 128), 0), 1.0 / 16, 0.0).astype(BF16)
    rstd = lax.rsqrt(dot(gather, high) + dot(gather, low) + EPS)
    return sums * jnp.concatenate([rstd] * (sums.shape[0] // 16), axis=0)


def usable_only(flags, start, atom_dev, count_ref):
    lanes = flags.shape[1]
    device = lax.axis_index("atom")
    position = device * atom_dev + start + iota((1, lanes), 1)
    count = jnp.broadcast_to(count_ref[0:1, 0:1], (1, lanes))
    return jnp.where(position < count, flags, 0.0)


def live_rows(flags, wanted, query_len, key_len, live_ref):
    total = flags.shape[1]
    flags8 = jnp.broadcast_to(flags, (8, total))
    rolled = {}
    for n, w in wanted:
        start = 128 + query_len * w - (key_len - query_len) // 2
        shift = start % 128
        if shift not in rolled:
            rolled[shift] = pltpu.roll(flags8, total - shift, 1)
        row = rolled[shift][0:1, start - shift : start - shift + key_len]
        live_ref[n : n + 1] = jnp.where(row > 0.5, 0.0, MASKED)


def early_kernel(
    count_ref,
    weight_ref,
    info_ref,
    pair_ref,
    cond_ref,
    atoms_ref,
    ada_hbm,
    ada_b_ref,
    zero_hbm,
    zero_b_ref,
    qkvg_hbm,
    query_b_ref,
    bias_ref,
    lhs_ref,
    scale0,
    shift0,
    scale1,
    shift1,
    gate0,
    gate1,
    k_ref,
    v_ref,
    q_ref,
    gate_ref,
    wqg_ref,
    ada_w_ref,
    zero_w_ref,
    qkvg_ref,
    sum_ref,
    half_ref,
    live_ref,
    norm_ref,
    attn_ref,
    sems,
):
    fetches = [
        pltpu.make_async_copy(src, dst, sems.at[n])
        for n, (src, dst) in enumerate(
            ((ada_hbm, ada_w_ref), (zero_hbm, zero_w_ref), (qkvg_hbm, qkvg_ref))
        )
    ]
    for c in fetches:
        c.start()
    heads = weight_ref.shape[0]
    windows, score_rows, key_len = bias_ref.shape
    query_len = score_rows // heads
    pair_lhs(weight_ref, lhs_ref)
    ones = jnp.ones((1, 128), F32)
    flags = jnp.concatenate([ones, usable_only(info_ref[0:1], 0, info_ref.shape[1], count_ref), ones], axis=1)
    live_rows(flags, [(w, w) for w in range(windows)], query_len, key_len, live_ref)
    per = query_len // 16
    n = 16 * heads

    def first(c):
        x = pair_ref[c // per, c % per * 256 : c % per * 256 + 256]
        sum_ref[c % 4], half_ref[c % 4, 0], half_ref[c % 4, 1] = pair_sums(
            x, lhs_ref[...], heads
        )

    def second(c):
        got = pair_scale(sum_ref[c % 4], half_ref[c % 4, 0], half_ref[c % 4, 1])
        w = c // per
        live = live_ref[w : w + 1]
        for h in range(heads):
            at = h * query_len + c % per * 16
            bias_ref[w, at : at + 16] = got[h * 16 : h * 16 + 16] + live

    atom_dev, width = cond_ref.shape
    factor = (width // heads) ** (-0.5)

    def cond_piece(lo, hi):
        norm_ref[lo:hi], scale0[lo:hi], shift0[lo:hi] = cond_rows(
            cond_ref[lo:hi], ada_w_ref, ada_b_ref
        )

    def adapt_piece(lo, hi):
        scale1[lo:hi], shift1[lo:hi] = adapt_rows(norm_ref[lo:hi], ada_w_ref, ada_b_ref)

    def zero_piece(lo, hi):
        gate0[lo:hi], gate1[lo:hi] = zero_rows(norm_ref[lo:hi], zero_w_ref, zero_b_ref)

    def attn_piece(lo, hi):
        attn_ref[lo:hi] = attn_rows(atoms_ref[0, lo:hi], scale0[lo:hi], shift0[lo:hi])

    def keyval_piece(lo, hi):
        k_ref[lo:hi], v_ref[lo:hi] = keyval_rows(attn_ref[lo:hi], qkvg_ref)

    def query_piece(lo, hi):
        q_ref[lo:hi], gate_ref[lo:hi] = query_rows(
            attn_ref[lo:hi], wqg_ref, query_b_ref, factor
        )

    own = (cond_piece, adapt_piece, zero_piece, attn_piece, keyval_piece, query_piece)
    chunks = range(windows * per)
    steps = skew([lambda c=c: first(c) for c in chunks], [lambda c=c: second(c) for c in chunks])
    lead = len(steps) * 2 // 5
    weave(steps[:lead])
    for c in fetches:
        c.wait()
    wqg_ref[:, :width] = qkvg_ref[:, :width]
    wqg_ref[:, width:] = qkvg_ref[:, 3 * width :]
    weave(steps[lead:], skew(*[each(f, atom_dev, 3) for f in own]))


def cond_rows(x, ada_w_ref, ada_b_ref):
    norm = norm_rows(x.astype(F32)).astype(BF16)
    adapt = dot(norm, ada_w_ref[0])
    width = norm.shape[1]
    return norm, sigmoid(adapt[:, :width] + ada_b_ref[0:1]), adapt[:, width:]


def adapt_rows(norm, ada_w_ref, ada_b_ref):
    adapt = dot(norm, ada_w_ref[1])
    width = norm.shape[1]
    return sigmoid(adapt[:, :width] + ada_b_ref[1:2]), adapt[:, width:]


def zero_rows(norm, zero_w_ref, zero_b_ref):
    return [sigmoid(dot(norm, zero_w_ref[u]) + zero_b_ref[u : u + 1]) for u in range(2)]


def attn_rows(x, scale, shift):
    return (norm_rows(x.astype(F32)) * scale + shift).astype(BF16)


def keyval_rows(attn, qkvg_ref):
    width = attn.shape[1]
    y = dot(attn, qkvg_ref[:, width : 3 * width]).astype(BF16)
    return y[:, :width], y[:, width:]


def query_rows(attn, wqg_ref, query_b_ref, factor):
    width = attn.shape[1]
    y = dot(attn, wqg_ref[...])
    return ((y[:, :width] + query_b_ref[0:1]) * factor).astype(BF16), sigmoid(y[:, width:])


def each(step, n, pieces):
    size = -(-n // pieces // 16) * 16
    return [lambda lo=lo, hi=min(n, lo + size): step(lo, hi) for lo in range(0, n, size)]


PIECES = 2


def weave(*streams):
    steps = [x for x in streams if x]
    total = max(len(x) for x in steps)
    done = [0] * len(steps)
    for t in range(total):
        for n, x in enumerate(steps):
            while done[n] * total < (t + 1) * len(x) and done[n] < len(x):
                x[done[n]]()
                done[n] += 1


def skew(*stages):
    pieces = len(stages[0])
    out = []
    for t in range(pieces + len(stages) - 1):
        for n, stage in enumerate(stages):
            if 0 <= t - n < pieces:
                out.append(stage[t - n])
    return out


def block_kernel(
    atoms_ref,
    count_ref,
    info_ref,
    across_ref,
    within_ref,
    bias_ref,
    lhs_ref,
    scale0_own,
    shift0_own,
    scale1_own,
    shift1_own,
    gate0_own,
    gate1_own,
    k_own,
    v_own,
    q_own,
    gate_own,
    wqg_ref,
    ada_w_ref,
    ada_b_ref,
    zero_w_ref,
    zero_b_ref,
    qkvg_ref,
    query_b_ref,
    out_w_ref,
    swiglu_ref,
    down_ref,
    token_w_ref,
    atoms_hbm,
    tokens_hbm,
    scale0,
    shift0,
    scale1,
    shift1,
    gate0,
    gate1,
    edge_bias,
    live_ref,
    onehot_ref,
    inverse_ref,
    left_ref,
    right_ref,
    attn_ref,
    q_ref,
    k_ref,
    v_ref,
    gate_ref,
    score_ref,
    prob_ref,
    total_ref,
    blend_ref,
    after_ref,
    trans_ref,
    hidden_ref,
    result_ref,
    feature_ref,
    tokens_ref,
    sems,
):
    samples, atom_dev, width = atoms_ref.shape
    windows, score_rows, key_len = bias_ref.shape
    query_len = atom_dev // windows
    heads = score_rows // query_len
    head_dim = width // heads
    margin = (key_len - query_len) // 2
    tok_dev = atom_dev // ATOMS_PER_TOKEN
    ext = atom_dev + 2 * HALO
    rows = atom_dev + 2 * EDGE
    first = HALO - EDGE
    hidden = down_ref.shape[0]
    token_width = token_w_ref.shape[1]
    factor = head_dim ** (-0.5)

    odd = lax.axis_index("atom") % 2 == 1
    left_ref[...] = jnp.where(odd, within_ref[...], across_ref[...])
    right_ref[...] = jnp.where(odd, across_ref[...], within_ref[...])
    at = samples * HALO
    at += HALO + EDGE_Q * 16
    exists = info_ref[0:1]
    own = info_ref[1:2]
    info_l = left_ref[at : at + 16].astype(F32)
    info_r = right_ref[at : at + 16].astype(F32)
    flags = jnp.concatenate([info_l[0:1], exists, info_r[0:1]], axis=1)
    flags = usable_only(flags, -128, atom_dev, count_ref)
    tokens = jnp.concatenate([info_l[1:2] - tok_dev, own, info_r[1:2] + tok_dev], axis=1)
    total = flags.shape[1]
    lane = iota((1, total), 1)
    halo = jnp.where((lane >= 128) & (lane < 128 + atom_dev), 1.0, flags)
    inner = [(w + 1, w) for w in (0, 1, windows - 2, windows - 1)]
    live_rows(halo, inner, query_len, key_len, live_ref)
    outer = [(w + 1, w) for w in (-1, windows)]
    live_rows(flags, outer, query_len, key_len, live_ref)
    flags8 = jnp.broadcast_to(flags, (8, total))
    shift = 128 - EDGE
    flags = pltpu.roll(flags8, total - shift, 1)[0:1]
    tokens = pltpu.roll(jnp.broadcast_to(tokens, (8, total)), total - shift, 1)[0:1]
    lanes = onehot_ref.shape[1]
    slot = iota((tok_dev, lanes), 0).astype(F32)
    inside = iota((tok_dev, lanes), 1) < rows
    hit = (tokens[:, :lanes] == slot) & (flags[:, :lanes] > 0.5) & inside
    onehot = jnp.where(hit, 1.0, 0.0)
    onehot_ref[...] = onehot.astype(BF16)
    counts = jnp.sum(onehot, -1, keepdims=True)
    inverse_ref[...] = jnp.broadcast_to(1.0 / jnp.maximum(counts, 1.0), inverse_ref.shape)

    lane_head = iota((1, width), 1) // head_dim
    masks = [jnp.where(lane_head == h, 1.0, 0.0).astype(BF16) for h in range(heads)]
    places = [
        (EDGE + w * query_len, query_len, HALO + w * query_len - margin, w)
        for w in range(windows)
    ]
    for w, r in ((-1, EDGE - EDGE_Q), (windows, EDGE + atom_dev)):
        places.append((r, EDGE_Q, HALO + w * query_len - margin, w))

    def spliced(middle, off, lo, hi):
        parts = []
        for base, size, ref, start in (
            (0, HALO, left_ref, off),
            (HALO, atom_dev, middle, 0),
            (HALO + atom_dev, HALO, right_ref, off),
        ):
            x, y = max(lo, base), min(hi, base + size)
            if x < y:
                parts.append(ref[x - base + start : y - base + start])
        return parts[0] if len(parts) == 1 else jnp.concatenate(parts, axis=0)

    def stream_rows(s, lo, hi):
        return spliced(atoms_ref.at[s], s * HALO, lo, hi)

    def join(own, halo, lo, hi):
        side = halo.shape[0] // 2
        parts = []
        for base, size, ref, start in (
            (0, side, halo, 0),
            (side, atom_dev, own, 0),
            (side + atom_dev, side, halo, side),
        ):
            x, y = max(lo, base), min(hi, base + size)
            if x < y:
                parts.append(ref[x - base + start : y - base + start])
        return parts[0] if len(parts) == 1 else jnp.concatenate(parts, axis=0)

    def halos(off):
        return jnp.concatenate([left_ref[off : off + HALO], right_ref[off : off + HALO]], axis=0)

    def lead():
        def cond_step():
            norm, scale0[...], shift0[...] = cond_rows(
                halos(samples * HALO), ada_w_ref, ada_b_ref
            )
            norm = norm[first : first + 2 * EDGE]
            scale1[...], shift1[...] = adapt_rows(norm, ada_w_ref, ada_b_ref)
            gate0[...], gate1[...] = zero_rows(norm, zero_w_ref, zero_b_ref)

        def attn_step():
            attn = attn_rows(halos(0), scale0[...], shift0[...])
            k, v = keyval_rows(attn, qkvg_ref)
            end = HALO + atom_dev
            k_ref[0, :HALO], k_ref[0, end:] = k[:HALO], k[HALO:]
            v_ref[0, :HALO], v_ref[0, end:] = v[:HALO], v[HALO:]
            q, gate = query_rows(attn[first : first + 2 * EDGE], wqg_ref, query_b_ref, factor)
            end = EDGE + atom_dev
            q_ref[0, :EDGE], q_ref[0, end:] = q[:EDGE], q[EDGE:]
            gate_ref[0, :EDGE], gate_ref[0, end:] = gate[:EDGE], gate[EDGE:]

        def copy_step():
            k_ref[0, HALO : HALO + atom_dev] = k_own[...]
            v_ref[0, HALO : HALO + atom_dev] = v_own[...]
            q_ref[0, EDGE : EDGE + atom_dev] = q_own[...]
            gate_ref[0, EDGE : EDGE + atom_dev] = gate_own[...]

        def edge_step(e):
            x = (left_ref, right_ref)[e]
            start = (samples + 1) * HALO
            x = x[start : start + EDGE_Q * 16]
            x = jnp.concatenate([x, jnp.zeros_like(x)], axis=0)
            got = pair_scale(*pair_sums(x, lhs_ref[...], heads))
            for h in range(heads):
                edge_bias[e, h * EDGE_Q : (h + 1) * EDGE_Q] = got[h * 16 : h * 16 + EDGE_Q]

        return [copy_step, cond_step, attn_step] + [lambda e=e: edge_step(e) for e in range(2)]

    def prepare(s):
        def norm_piece(lo, hi):
            attn_ref[s, lo:hi] = attn_rows(
                stream_rows(s, lo, hi),
                join(scale0_own, scale0, lo, hi),
                join(shift0_own, shift0, lo, hi),
            )

        def keyval_piece(lo, hi):
            k_ref[s, lo:hi], v_ref[s, lo:hi] = keyval_rows(attn_ref[s, lo:hi], qkvg_ref)

        def query_piece(lo, hi):
            lo, hi = max(lo - first, 0), min(hi - first, rows)
            q_ref[s, lo:hi], gate_ref[s, lo:hi] = query_rows(
                attn_ref[s, first + lo : first + hi], wqg_ref, query_b_ref, factor
            )

        return skew(*[each(f, ext, 4) for f in (norm_piece, keyval_piece, query_piece)])

    def attend(s):
        def score(t):
            r, n, key, w = places[t]
            if n >= 16:
                q = q_ref[s, r : r + n]
                wide = jnp.concatenate([q * masks[h] for h in range(heads)], axis=0)
                bias = bias_ref[w]
            else:
                base = r // 16 * 16
                q = q_ref[s, base : base + 16].astype(F32)[r - base : r - base + n]
                wide = jnp.concatenate(
                    [jnp.where(lane_head == h, q, 0.0) for h in range(heads)], axis=0
                ).astype(BF16)
                bias = edge_bias[0 if w < 0 else 1]
            got = dot_t(wide, k_ref[s, key : key + key_len])
            if 1 < w < windows - 2:
                got = got + bias
            else:
                got = got + (bias + live_ref[w + 1 : w + 2])
            score_ref[s % 2, t, : heads * n] = got

        def soften(t):
            n = heads * places[t][1]
            x = score_ref[s % 2, t, :n]
            weights = jnp.exp(x - jnp.max(x, -1, keepdims=True))
            prob_ref[s % 2, t, :n] = weights.astype(BF16)
            sums = jnp.sum(weights, -1, keepdims=True)
            n = places[t][1]
            pick = jnp.broadcast_to(sums[0:n], (n, width))
            for h in range(1, heads):
                pick = jnp.where(lane_head == h, sums[h * n : (h + 1) * n], pick)
            total_ref[s % 2, t, :n] = pick

        def blend(t):
            r, n, key, w = places[t]
            out = dot(prob_ref[s % 2, t, : heads * n], v_ref[s, key : key + key_len])
            pick = out[0:n]
            for h in range(1, heads):
                pick = jnp.where(lane_head == h, out[h * n : (h + 1) * n], pick)
            got = pick / total_ref[s % 2, t, :n] * gate_ref[s, r : r + n]
            if n < 16:
                pad = jnp.zeros_like(got)
                base = r // 16 * 16
                got = jnp.concatenate([pad, got] if r > base else [got, pad], axis=0)
                r, n = base, 16
            blend_ref[s, r : r + n] = got.astype(BF16)

        count = len(places)
        out = []
        for t in range(count + 4):
            if t < count:
                out.append(lambda t=t: score(t))
            if 0 <= t - 2 < count:
                out.append(lambda t=t: soften(t - 2))
            if 0 <= t - 4 < count:
                out.append(lambda t=t: blend(t - 4))
        return out

    def atom_copy(s):
        src = result_ref.at[s, pl.ds(EDGE, atom_dev)]
        return pltpu.make_async_copy(src, atoms_hbm.at[s], sems.at[0, s])

    def token_copy(s, n):
        lanes = pl.ds(n * 256, 256)
        return pltpu.make_async_copy(
            tokens_ref.at[s, :, lanes], tokens_hbm.at[s, :, lanes], sems.at[1 + n, s]
        )

    token_steps = token_width // 256

    def finish(s):
        def after_piece(lo, hi):
            x = stream_rows(s, first + lo, first + hi).astype(F32)
            y = (x + join(gate0_own, gate0, lo, hi) * dot(blend_ref[s, lo:hi], out_w_ref[...])).astype(BF16)
            after_ref[s, lo:hi] = y
            trans_ref[s, lo:hi] = attn_rows(
                y, join(scale1_own, scale1, lo, hi), join(shift1_own, shift1, lo, hi)
            )

        def hidden_piece(lo, hi):
            y = dot(trans_ref[s, lo:hi], swiglu_ref[...])
            a = y[:, :hidden]
            hidden_ref[s, lo:hi] = (a * sigmoid(a) * y[:, hidden:]).astype(BF16)

        def result_piece(lo, hi):
            y = join(gate1_own, gate1, lo, hi) * dot(hidden_ref[s, lo:hi], down_ref[...])
            result_ref[s, lo:hi] = (after_ref[s, lo:hi].astype(F32) + y).astype(BF16)

        def feature_piece(lo, hi):
            y = dot(result_ref[s, lo:hi], token_w_ref[...])
            feature_ref[s % 2, lo:hi] = jnp.maximum(y, 0.0).astype(BF16)

        def token_piece(lo, hi):
            y = dot(onehot_ref[:, :rows], feature_ref[s % 2, :, lo:hi])
            for c in range(lo, hi, 128):
                z = y[:, c - lo : c - lo + 128] * inverse_ref[...]
                tokens_ref[s, :, c : c + 128] = z.astype(BF16)
            token_copy(s, lo // 256).start()

        stages = (after_piece, hidden_piece, result_piece, feature_piece)
        out = skew(*[each(f, rows, PIECES) for f in stages])
        out.append(lambda: atom_copy(s).start())
        out += [lambda lo=lo: token_piece(lo, lo + 256) for lo in range(0, token_width, 256)]
        return out

    weave(lead())
    for s in range(samples):
        weave(
            attend(s),
            finish(s - 1) if s > 0 else None,
            prepare(s + 1) if s + 1 < samples else None,
        )
    weave(finish(samples - 1))
    for s in range(samples):
        atom_copy(s).wait()
        for n in range(token_steps):
            token_copy(s, n).wait()


def on_device(
    atoms_in,
    cond,
    pair,
    atom_mask,
    atom_count,
    atom_to_token,
    ada_weight,
    ada_bias,
    zero_weight,
    zero_bias,
    qkvg_weight,
    query_bias,
    pair_weight,
    out_weight,
    swiglu_weight,
    down_weight,
    token_weight,
):
    samples, atom_dev, width = atoms_in.shape
    windows, query_len, channels, key_len = pair.shape
    count_row = jnp.broadcast_to(atom_count, (8, 128))
    heads = pair_weight.shape[0]
    hidden = down_weight.shape[0]
    token_width = token_weight.shape[1]
    tok_dev = atom_dev // ATOMS_PER_TOKEN
    ext = atom_dev + 2 * HALO
    rows = atom_dev + 2 * EDGE
    far = pl.BlockSpec(memory_space=pltpu.HBM)
    vmem = pl.BlockSpec(memory_space=pltpu.VMEM)

    def near(array):
        return pltpu.with_memory_space_constraint(array, pltpu.VMEM)

    def away(array):
        return pltpu.with_memory_space_constraint(array, pltpu.HBM)

    wire_rows = (samples + 1) * HALO + EDGE_Q * channels + 16
    wire = pltpu.VMEM((wire_rows, width), BF16)
    pair = pair.reshape(windows, query_len * channels, key_len)
    across, within, info = pl.pallas_call(
        pack_kernel,
        out_shape=(wire, wire, pltpu.VMEM((16, atom_dev), F32)),
        in_specs=[far] * 5,
        out_specs=(vmem, vmem, vmem),
        scratch_shapes=[
            pltpu.VMEM((atom_dev,), jnp.int32),
            pltpu.VMEM((atom_dev,), jnp.int32),
            pltpu.SemaphoreType.DMA((2 * (samples + 3),)),
        ],
        compiler_params=pltpu.CompilerParams(vmem_limit_bytes=4 << 20),
        name="pack",
    )(*[away(a) for a in (atom_mask, atom_to_token, atoms_in, cond, pair)])
    count = lax.axis_size("atom")
    swaps = [[(i, i + 1) for i in range(at, count - 1, 2)] for at in (1, 0)]
    swaps = [pairs + [(j, i) for i, j in pairs] for pairs in swaps]
    across = lax.ppermute(across, "atom", swaps[0])
    within = lax.ppermute(within, "atom", swaps[1])

    lhs_shape = (3 * 16 * heads, 16 * channels)
    shared = [
        near(a)
        for a in (
            atoms_in,
            ada_bias,
            zero_bias,
            query_bias.reshape(1, width),
        )
    ]
    near_atoms, ada_b, zero_b, query_b = shared
    early_weights = (ada_weight, zero_weight, qkvg_weight)
    ada_w, zero_w, qkvg_w = [away(a) for a in early_weights]
    near_count = near(count_row)
    own_rows = pltpu.VMEM((atom_dev, width), F32)
    own_half = pltpu.VMEM((atom_dev, width), BF16)
    early = pl.pallas_call(
        early_kernel,
        out_shape=(
            pltpu.VMEM((windows, heads * query_len, key_len), F32),
            pltpu.VMEM(lhs_shape, BF16),
        )
        + (own_rows,) * 6
        + (own_half,) * 3
        + (own_rows, pltpu.VMEM((width, 2 * width), BF16))
        + tuple(pltpu.VMEM(a.shape, a.dtype) for a in early_weights),
        in_specs=[vmem] * 6 + [far, vmem, far, vmem, far, vmem],
        out_specs=(vmem,) * 16,
        scratch_shapes=[
            pltpu.VMEM((4, 16 * heads, key_len), F32),
            pltpu.VMEM((4, 2, 128, key_len), BF16),
            pltpu.VMEM((16, key_len), F32),
            pltpu.VMEM((atom_dev, width), BF16),
            pltpu.VMEM((atom_dev, width), BF16),
            pltpu.SemaphoreType.DMA((3,)),
        ],
        compiler_params=pltpu.CompilerParams(
            vmem_limit_bytes=8 << 20
        ),
        name="early",
    )(
        near_count, near(pair_weight), near(info), near(pair), near(cond), near_atoms,
        ada_w,
        ada_b,
        zero_w,
        zero_b,
        qkvg_w,
        query_b,
    )
    ada_w, zero_w, qkvg_w = [near(a) for a in early[13:]]
    first_weights = (ada_w, ada_b, zero_w, zero_b, qkvg_w, query_b)

    last_weights = [near(a) for a in (out_weight, swiglu_weight, down_weight, token_weight)]
    operands = [near_atoms, near_count] + [near(a) for a in (info, across, within, *early[:13])]
    operands += [*first_weights, *last_weights]
    return pl.pallas_call(
        block_kernel,
        out_shape=(
            jax.ShapeDtypeStruct((samples, atom_dev, width), BF16),
            jax.ShapeDtypeStruct((samples, tok_dev, token_width), BF16),
        ),
        in_specs=[vmem] * len(operands),
        out_specs=(far, far),
        scratch_shapes=[
            pltpu.VMEM((2 * HALO, width), F32),
            pltpu.VMEM((2 * HALO, width), F32),
            pltpu.VMEM((2 * EDGE, width), F32),
            pltpu.VMEM((2 * EDGE, width), F32),
            pltpu.VMEM((2 * EDGE, width), F32),
            pltpu.VMEM((2 * EDGE, width), F32),
            pltpu.VMEM((2, heads * EDGE_Q, key_len), F32),
            pltpu.VMEM((16, key_len), F32),
            pltpu.VMEM((tok_dev, 512), BF16),
            pltpu.VMEM((tok_dev, 128), F32),
            pltpu.VMEM((wire_rows, width), BF16),
            pltpu.VMEM((wire_rows, width), BF16),
            pltpu.VMEM((samples, ext, width), BF16),
            pltpu.VMEM((samples, rows, width), BF16),
            pltpu.VMEM((samples, ext, width), BF16),
            pltpu.VMEM((samples, ext, width), BF16),
            pltpu.VMEM((samples, rows, width), F32),
            pltpu.VMEM((2, windows + 2, heads * query_len, key_len), F32),
            pltpu.VMEM((2, windows + 2, heads * query_len, key_len), BF16),
            pltpu.VMEM((2, windows + 2, query_len, width), F32),
            pltpu.VMEM((samples, rows, width), BF16),
            pltpu.VMEM((samples, rows, width), BF16),
            pltpu.VMEM((samples, rows, width), BF16),
            pltpu.VMEM((samples, rows, hidden), BF16),
            pltpu.VMEM((samples, rows, width), BF16),
            pltpu.VMEM((2, rows, token_width), BF16),
            pltpu.VMEM((samples, tok_dev, token_width), BF16),
            pltpu.SemaphoreType.DMA((1 + token_width // 256, samples)),
        ],
        compiler_params=pltpu.CompilerParams(vmem_limit_bytes=24 << 20),
        name="block",
    )(*operands)


def solution(mesh):
    in_specs = (
        P("struct", "atom", None),
        P(("struct", "atom"), None),
        P(("struct", "atom"), None, None, None),
        P(("struct", "atom")),
        P("struct"),
        P(("struct", "atom")),
        P(),
        P(),
        P(),
        P(),
        P(),
        P(),
        P(),
        P(),
        P(),
        P(),
        P(),
    )
    out_specs = (P("struct", "atom", None), P("struct", "atom", None))
    return jax.shard_map(
        on_device, mesh=mesh, in_specs=in_specs, out_specs=out_specs, check_vma=False
    )
```

```python
import functools

import jax
import jax.numpy as jnp
from jax import lax
from jax.experimental import pallas as pl
from jax.experimental.pallas import tpu as pltpu
from jax.sharding import PartitionSpec as P

ATOMS_PER_TOKEN = 8
EPS = 1e-05
HALO = 80
EDGE = 16
EDGE_Q = 8
MASKED = -1e30
BF16 = jnp.bfloat16
F32 = jnp.float32


def dot(a, b):
    return jnp.dot(a, b, preferred_element_type=F32)


def dot_t(a, b):
    return lax.dot_general(a, b, (((1,), (1,)), ((), ())), preferred_element_type=F32)


def norm_rows(x):
    center = jnp.mean(x, -1, keepdims=True)
    off = x - center
    spread = jnp.mean(jnp.square(off), -1, keepdims=True)
    return off * lax.rsqrt(spread + EPS)


def sigmoid(x):
    return 0.5 * jnp.tanh(0.5 * x) + 0.5


def iota(shape, dim):
    return lax.broadcasted_iota(jnp.int32, shape, dim)


def pack_kernel(
    mask_hbm,
    token_hbm,
    atoms_ref,
    cond_ref,
    pair_ref,
    across_ref,
    within_ref,
    info_ref,
    mask_ref,
    token_ref,
    sems,
):
    samples, atom_dev, _ = atoms_ref.shape
    windows, pair_rows, _ = pair_ref.shape
    edge_rows = EDGE_Q * 16
    copies = []

    def copy(src, dst):
        c = pltpu.make_async_copy(src, dst, sems.at[len(copies)])
        c.start()
        copies.append(c)

    copy(mask_hbm, mask_ref)
    copy(token_hbm, token_ref)
    rows = (samples + 1) * HALO
    device = lax.axis_index("atom")
    odd = device % 2
    for wire, last in ((across_ref, odd), (within_ref, 1 - odd)):
        at = pl.multiple_of(last * (atom_dev - HALO), 16)
        w = last * (windows - 1)
        p = pl.multiple_of(last * (pair_rows - edge_rows), 16)
        for s in range(samples):
            copy(atoms_ref.at[s, pl.ds(at, HALO)], wire.at[pl.ds(s * HALO, HALO)])
        copy(cond_ref.at[pl.ds(at, HALO)], wire.at[pl.ds(samples * HALO, HALO)])
        copy(pair_ref.at[w, pl.ds(p, edge_rows)], wire.at[pl.ds(rows, edge_rows)])
    rows += edge_rows
    for c in copies[:2]:
        c.wait()
    mask = mask_ref[...].reshape(1, atom_dev)
    token = token_ref[...].reshape(1, atom_dev)
    exists = jnp.where(mask == 1, 1.0, 0.0)
    own = (token - device * (atom_dev // ATOMS_PER_TOKEN)).astype(F32)
    row = iota((16, atom_dev), 0)
    info = jnp.where(row == 0, exists, jnp.where(row == 1, own, 0.0))
    info_ref[...] = info
    end = info[:, atom_dev - 128 :]
    start = info[:, :128]
    across_ref[rows : rows + 16] = jnp.where(odd == 1, end, start).astype(BF16)
    within_ref[rows : rows + 16] = jnp.where(odd == 1, start, end).astype(BF16)
    for c in copies[2:]:
        c.wait()


def pair_lhs(weight_ref, lhs_ref):
    heads, channels = weight_ref.shape
    wide = 16 * channels
    w = weight_ref[...]
    w = w - jnp.mean(w, -1, keepdims=True)
    spread = jnp.where(iota((channels, wide), 1) % channels == iota((channels, wide), 0), 1.0, 0.0)
    tiled = jnp.dot(w, spread, precision=lax.Precision.HIGHEST, preferred_element_type=F32)
    full = jnp.concatenate(
        [jnp.broadcast_to(tiled[h : h + 1], (16, wide)) for h in range(heads)], axis=0
    )
    shape = (16 * heads, wide)
    full = jnp.where(iota(shape, 1) // channels == iota(shape, 0) % 16, full, 0.0)
    high = full.astype(BF16)
    rest = full - high.astype(F32)
    mid = rest.astype(BF16)
    low = (rest - mid.astype(F32)).astype(BF16)
    n = 16 * heads
    lhs_ref[0:n] = high
    lhs_ref[n : 2 * n] = mid
    lhs_ref[2 * n : 3 * n] = low


def pair_sums(x, lhs, heads):
    n = 16 * heads
    out = dot(lhs, x)
    rows = x.astype(F32).reshape(16, 16, -1)
    off = rows - jnp.mean(rows, axis=1, keepdims=True)
    square = off * off
    half = (square[:, :8] + square[:, 8:]).reshape(128, -1)
    high = half.astype(BF16)
    low = (half - high.astype(F32)).astype(BF16)
    sums = out[0:n] + out[n : 2 * n] + out[2 * n : 3 * n]
    return sums, high, low


def pair_scale(sums, high, low):
    gather = jnp.where(iota((16, 128), 1) // 8 == iota((16, 128), 0), 1.0 / 16, 0.0).astype(BF16)
    rstd = lax.rsqrt(dot(gather, high) + dot(gather, low) + EPS)
    return sums * jnp.concatenate([rstd] * (sums.shape[0] // 16), axis=0)


def usable_only(flags, start, atom_dev, count_ref):
    lanes = flags.shape[1]
    device = lax.axis_index("atom")
    position = device * atom_dev + start + iota((1, lanes), 1)
    count = jnp.broadcast_to(count_ref[0:1, 0:1], (1, lanes))
    return jnp.where(position < count, flags, 0.0)


def live_rows(flags, wanted, query_len, key_len, live_ref):
    total = flags.shape[1]
    flags8 = jnp.broadcast_to(flags, (8, total))
    rolled = {}
    for n, w in wanted:
        start = 128 + query_len * w - (key_len - query_len) // 2
        shift = start % 128
        if shift not in rolled:
            rolled[shift] = pltpu.roll(flags8, total - shift, 1)
        row = rolled[shift][0:1, start - shift : start - shift + key_len]
        live_ref[n : n + 1] = jnp.where(row > 0.5, 0.0, MASKED)


def early_kernel(
    count_ref,
    weight_ref,
    info_ref,
    pair_ref,
    cond_ref,
    atoms_ref,
    ada_hbm,
    ada_b_ref,
    zero_hbm,
    zero_b_ref,
    qkvg_hbm,
    query_b_ref,
    bias_ref,
    lhs_ref,
    scale0,
    shift0,
    scale1,
    shift1,
    gate0,
    gate1,
    k_ref,
    v_ref,
    q_ref,
    gate_ref,
    wqg_ref,
    ada_w_ref,
    zero_w_ref,
    qkvg_ref,
    sum_ref,
    half_ref,
    live_ref,
    norm_ref,
    attn_ref,
    sems,
):
    fetches = [
        pltpu.make_async_copy(src, dst, sems.at[n])
        for n, (src, dst) in enumerate(
            ((ada_hbm, ada_w_ref), (zero_hbm, zero_w_ref), (qkvg_hbm, qkvg_ref))
        )
    ]
    for c in fetches:
        c.start()
    heads = weight_ref.shape[0]
    windows, score_rows, key_len = bias_ref.shape
    query_len = score_rows // heads
    pair_lhs(weight_ref, lhs_ref)
    ones = jnp.ones((1, 128), F32)
    flags = jnp.concatenate([ones, usable_only(info_ref[0:1], 0, info_ref.shape[1], count_ref), ones], axis=1)
    live_rows(flags, [(w, w) for w in range(windows)], query_len, key_len, live_ref)
    per = query_len // 16
    n = 16 * heads

    def first(c):
        x = pair_ref[c // per, c % per * 256 : c % per * 256 + 256]
        sum_ref[c % 4], half_ref[c % 4, 0], half_ref[c % 4, 1] = pair_sums(
            x, lhs_ref[...], heads
        )

    def second(c):
        got = pair_scale(sum_ref[c % 4], half_ref[c % 4, 0], half_ref[c % 4, 1])
        w = c // per
        live = live_ref[w : w + 1]
        for h in range(heads):
            at = h * query_len + c % per * 16
            bias_ref[w, at : at + 16] = got[h * 16 : h * 16 + 16] + live

    atom_dev, width = cond_ref.shape
    factor = (width // heads) ** (-0.5)

    def cond_piece(lo, hi):
        norm_ref[lo:hi], scale0[lo:hi], shift0[lo:hi] = cond_rows(
            cond_ref[lo:hi], ada_w_ref, ada_b_ref
        )

    def adapt_piece(lo, hi):
        scale1[lo:hi], shift1[lo:hi] = adapt_rows(norm_ref[lo:hi], ada_w_ref, ada_b_ref)

    def zero_piece(lo, hi):
        gate0[lo:hi], gate1[lo:hi] = zero_rows(norm_ref[lo:hi], zero_w_ref, zero_b_ref)

    def attn_piece(lo, hi):
        attn_ref[lo:hi] = attn_rows(atoms_ref[0, lo:hi], scale0[lo:hi], shift0[lo:hi])

    def keyval_piece(lo, hi):
        k_ref[lo:hi], v_ref[lo:hi] = keyval_rows(attn_ref[lo:hi], qkvg_ref)

    def query_piece(lo, hi):
        q_ref[lo:hi], gate_ref[lo:hi] = query_rows(
            attn_ref[lo:hi], wqg_ref, query_b_ref, factor
        )

    own = (cond_piece, adapt_piece, zero_piece, attn_piece, keyval_piece, query_piece)
    chunks = range(windows * per)
    steps = skew([lambda c=c: first(c) for c in chunks], [lambda c=c: second(c) for c in chunks])
    lead = len(steps) * 2 // 5
    weave(steps[:lead])
    for c in fetches:
        c.wait()
    wqg_ref[:, :width] = qkvg_ref[:, :width]
    wqg_ref[:, width:] = qkvg_ref[:, 3 * width :]
    weave(steps[lead:], skew(*[each(f, atom_dev, 3) for f in own]))


def cond_rows(x, ada_w_ref, ada_b_ref):
    norm = norm_rows(x.astype(F32)).astype(BF16)
    adapt = dot(norm, ada_w_ref[0])
    width = norm.shape[1]
    return norm, sigmoid(adapt[:, :width] + ada_b_ref[0:1]), adapt[:, width:]


def adapt_rows(norm, ada_w_ref, ada_b_ref):
    adapt = dot(norm, ada_w_ref[1])
    width = norm.shape[1]
    return sigmoid(adapt[:, :width] + ada_b_ref[1:2]), adapt[:, width:]


def zero_rows(norm, zero_w_ref, zero_b_ref):
    return [sigmoid(dot(norm, zero_w_ref[u]) + zero_b_ref[u : u + 1]) for u in range(2)]


def attn_rows(x, scale, shift):
    return (norm_rows(x.astype(F32)) * scale + shift).astype(BF16)


def keyval_rows(attn, qkvg_ref):
    width = attn.shape[1]
    y = dot(attn, qkvg_ref[:, width : 3 * width]).astype(BF16)
    return y[:, :width], y[:, width:]


def query_rows(attn, wqg_ref, query_b_ref, factor):
    width = attn.shape[1]
    y = dot(attn, wqg_ref[...])
    return ((y[:, :width] + query_b_ref[0:1]) * factor).astype(BF16), sigmoid(y[:, width:])


def each(step, n, pieces):
    size = -(-n // pieces // 16) * 16
    return [lambda lo=lo, hi=min(n, lo + size): step(lo, hi) for lo in range(0, n, size)]


PIECES = 2


def weave(*streams):
    steps = [x for x in streams if x]
    total = max(len(x) for x in steps)
    done = [0] * len(steps)
    for t in range(total):
        for n, x in enumerate(steps):
            while done[n] * total < (t + 1) * len(x) and done[n] < len(x):
                x[done[n]]()
                done[n] += 1


def skew(*stages):
    pieces = len(stages[0])
    out = []
    for t in range(pieces + len(stages) - 1):
        for n, stage in enumerate(stages):
            if 0 <= t - n < pieces:
                out.append(stage[t - n])
    return out


def block_kernel(
    atoms_ref,
    count_ref,
    info_ref,
    across_ref,
    within_ref,
    bias_ref,
    lhs_ref,
    scale0_own,
    shift0_own,
    scale1_own,
    shift1_own,
    gate0_own,
    gate1_own,
    k_own,
    v_own,
    q_own,
    gate_own,
    wqg_ref,
    ada_w_ref,
    ada_b_ref,
    zero_w_ref,
    zero_b_ref,
    qkvg_ref,
    query_b_ref,
    out_w_ref,
    swiglu_ref,
    down_ref,
    token_w_ref,
    atoms_hbm,
    tokens_hbm,
    scale0,
    shift0,
    scale1,
    shift1,
    gate0,
    gate1,
    edge_bias,
    live_ref,
    onehot_ref,
    inverse_ref,
    left_ref,
    right_ref,
    attn_ref,
    q_ref,
    k_ref,
    v_ref,
    gate_ref,
    score_ref,
    prob_ref,
    total_ref,
    blend_ref,
    after_ref,
    trans_ref,
    hidden_ref,
    result_ref,
    feature_ref,
    tokens_ref,
    sems,
):
    samples, atom_dev, width = atoms_ref.shape
    windows, score_rows, key_len = bias_ref.shape
    query_len = atom_dev // windows
    heads = score_rows // query_len
    head_dim = width // heads
    margin = (key_len - query_len) // 2
    tok_dev = atom_dev // ATOMS_PER_TOKEN
    ext = atom_dev + 2 * HALO
    rows = atom_dev + 2 * EDGE
    first = HALO - EDGE
    hidden = down_ref.shape[0]
    token_width = token_w_ref.shape[1]
    factor = head_dim ** (-0.5)

    odd = lax.axis_index("atom") % 2 == 1
    left_ref[...] = jnp.where(odd, within_ref[...], across_ref[...])
    right_ref[...] = jnp.where(odd, across_ref[...], within_ref[...])
    at = samples * HALO
    at += HALO + EDGE_Q * 16
    exists = info_ref[0:1]
    own = info_ref[1:2]
    info_l = left_ref[at : at + 16].astype(F32)
    info_r = right_ref[at : at + 16].astype(F32)
    flags = jnp.concatenate([info_l[0:1], exists, info_r[0:1]], axis=1)
    flags = usable_only(flags, -128, atom_dev, count_ref)
    tokens = jnp.concatenate([info_l[1:2] - tok_dev, own, info_r[1:2] + tok_dev], axis=1)
    total = flags.shape[1]
    lane = iota((1, total), 1)
    halo = jnp.where((lane >= 128) & (lane < 128 + atom_dev), 1.0, flags)
    inner = [(w + 1, w) for w in (0, 1, windows - 2, windows - 1)]
    live_rows(halo, inner, query_len, key_len, live_ref)
    outer = [(w + 1, w) for w in (-1, windows)]
    live_rows(flags, outer, query_len, key_len, live_ref)
    flags8 = jnp.broadcast_to(flags, (8, total))
    shift = 128 - EDGE
    flags = pltpu.roll(flags8, total - shift, 1)[0:1]
    tokens = pltpu.roll(jnp.broadcast_to(tokens, (8, total)), total - shift, 1)[0:1]
    lanes = onehot_ref.shape[1]
    slot = iota((tok_dev, lanes), 0).astype(F32)
    inside = iota((tok_dev, lanes), 1) < rows
    hit = (tokens[:, :lanes] == slot) & (flags[:, :lanes] > 0.5) & inside
    onehot = jnp.where(hit, 1.0, 0.0)
    onehot_ref[...] = onehot.astype(BF16)
    counts = jnp.sum(onehot, -1, keepdims=True)
    inverse_ref[...] = jnp.broadcast_to(1.0 / jnp.maximum(counts, 1.0), inverse_ref.shape)

    lane_head = iota((1, width), 1) // head_dim
    masks = [jnp.where(lane_head == h, 1.0, 0.0).astype(BF16) for h in range(heads)]
    places = [
        (EDGE + w * query_len, query_len, HALO + w * query_len - margin, w)
        for w in range(windows)
    ]
    for w, r in ((-1, EDGE - EDGE_Q), (windows, EDGE + atom_dev)):
        places.append((r, EDGE_Q, HALO + w * query_len - margin, w))

    def spliced(middle, off, lo, hi):
        parts = []
        for base, size, ref, start in (
            (0, HALO, left_ref, off),
            (HALO, atom_dev, middle, 0),
            (HALO + atom_dev, HALO, right_ref, off),
        ):
            x, y = max(lo, base), min(hi, base + size)
            if x < y:
                parts.append(ref[x - base + start : y - base + start])
        return parts[0] if len(parts) == 1 else jnp.concatenate(parts, axis=0)

    def stream_rows(s, lo, hi):
        return spliced(atoms_ref.at[s], s * HALO, lo, hi)

    def join(own, halo, lo, hi):
        side = halo.shape[0] // 2
        parts = []
        for base, size, ref, start in (
            (0, side, halo, 0),
            (side, atom_dev, own, 0),
            (side + atom_dev, side, halo, side),
        ):
            x, y = max(lo, base), min(hi, base + size)
            if x < y:
                parts.append(ref[x - base + start : y - base + start])
        return parts[0] if len(parts) == 1 else jnp.concatenate(parts, axis=0)

    def halos(off):
        return jnp.concatenate([left_ref[off : off + HALO], right_ref[off : off + HALO]], axis=0)

    def lead():
        def cond_step():
            norm, scale0[...], shift0[...] = cond_rows(
                halos(samples * HALO), ada_w_ref, ada_b_ref
            )
            norm = norm[first : first + 2 * EDGE]
            scale1[...], shift1[...] = adapt_rows(norm, ada_w_ref, ada_b_ref)
            gate0[...], gate1[...] = zero_rows(norm, zero_w_ref, zero_b_ref)

        def attn_step():
            attn = attn_rows(halos(0), scale0[...], shift0[...])
            k, v = keyval_rows(attn, qkvg_ref)
            end = HALO + atom_dev
            k_ref[0, :HALO], k_ref[0, end:] = k[:HALO], k[HALO:]
            v_ref[0, :HALO], v_ref[0, end:] = v[:HALO], v[HALO:]
            q, gate = query_rows(attn[first : first + 2 * EDGE], wqg_ref, query_b_ref, factor)
            end = EDGE + atom_dev
            q_ref[0, :EDGE], q_ref[0, end:] = q[:EDGE], q[EDGE:]
            gate_ref[0, :EDGE], gate_ref[0, end:] = gate[:EDGE], gate[EDGE:]

        def copy_step():
            k_ref[0, HALO : HALO + atom_dev] = k_own[...]
            v_ref[0, HALO : HALO + atom_dev] = v_own[...]
            q_ref[0, EDGE : EDGE + atom_dev] = q_own[...]
            gate_ref[0, EDGE : EDGE + atom_dev] = gate_own[...]

        def edge_step(e):
            x = (left_ref, right_ref)[e]
            start = (samples + 1) * HALO
            x = x[start : start + EDGE_Q * 16]
            x = jnp.concatenate([x, jnp.zeros_like(x)], axis=0)
            got = pair_scale(*pair_sums(x, lhs_ref[...], heads))
            for h in range(heads):
                edge_bias[e, h * EDGE_Q : (h + 1) * EDGE_Q] = got[h * 16 : h * 16 + EDGE_Q]

        return [copy_step, cond_step, attn_step] + [lambda e=e: edge_step(e) for e in range(2)]

    def prepare(s):
        def norm_piece(lo, hi):
            attn_ref[s, lo:hi] = attn_rows(
                stream_rows(s, lo, hi),
                join(scale0_own, scale0, lo, hi),
                join(shift0_own, shift0, lo, hi),
            )

        def keyval_piece(lo, hi):
            k_ref[s, lo:hi], v_ref[s, lo:hi] = keyval_rows(attn_ref[s, lo:hi], qkvg_ref)

        def query_piece(lo, hi):
            lo, hi = max(lo - first, 0), min(hi - first, rows)
            q_ref[s, lo:hi], gate_ref[s, lo:hi] = query_rows(
                attn_ref[s, first + lo : first + hi], wqg_ref, query_b_ref, factor
            )

        return skew(*[each(f, ext, 4) for f in (norm_piece, keyval_piece, query_piece)])

    def attend(s):
        def score(t):
            r, n, key, w = places[t]
            if n >= 16:
                q = q_ref[s, r : r + n]
                wide = jnp.concatenate([q * masks[h] for h in range(heads)], axis=0)
                bias = bias_ref[w]
            else:
                base = r // 16 * 16
                q = q_ref[s, base : base + 16].astype(F32)[r - base : r - base + n]
                wide = jnp.concatenate(
                    [jnp.where(lane_head == h, q, 0.0) for h in range(heads)], axis=0
                ).astype(BF16)
                bias = edge_bias[0 if w < 0 else 1]
            got = dot_t(wide, k_ref[s, key : key + key_len])
            if 1 < w < windows - 2:
                got = got + bias
            else:
                got = got + (bias + live_ref[w + 1 : w + 2])
            score_ref[s % 2, t, : heads * n] = got

        def soften(t):
            n = heads * places[t][1]
            x = score_ref[s % 2, t, :n]
            weights = jnp.exp(x - jnp.max(x, -1, keepdims=True))
            prob_ref[s % 2, t, :n] = weights.astype(BF16)
            sums = jnp.sum(weights, -1, keepdims=True)
            n = places[t][1]
            pick = jnp.broadcast_to(sums[0:n], (n, width))
            for h in range(1, heads):
                pick = jnp.where(lane_head == h, sums[h * n : (h + 1) * n], pick)
            total_ref[s % 2, t, :n] = pick

        def blend(t):
            r, n, key, w = places[t]
            out = dot(prob_ref[s % 2, t, : heads * n], v_ref[s, key : key + key_len])
            pick = out[0:n]
            for h in range(1, heads):
                pick = jnp.where(lane_head == h, out[h * n : (h + 1) * n], pick)
            got = pick / total_ref[s % 2, t, :n] * gate_ref[s, r : r + n]
            if n < 16:
                pad = jnp.zeros_like(got)
                base = r // 16 * 16
                got = jnp.concatenate([pad, got] if r > base else [got, pad], axis=0)
                r, n = base, 16
            blend_ref[s, r : r + n] = got.astype(BF16)

        count = len(places)
        out = []
        for t in range(count + 8):
            if t < count:
                out.append(lambda t=t: score(t))
            if 0 <= t - 4 < count:
                out.append(lambda t=t: soften(t - 4))
            if 0 <= t - 8 < count:
                out.append(lambda t=t: blend(t - 8))
        return out

    def atom_copy(s):
        src = result_ref.at[s, pl.ds(EDGE, atom_dev)]
        return pltpu.make_async_copy(src, atoms_hbm.at[s], sems.at[0, s])

    def token_copy(s, n):
        lanes = pl.ds(n * 256, 256)
        return pltpu.make_async_copy(
            tokens_ref.at[s, :, lanes], tokens_hbm.at[s, :, lanes], sems.at[1 + n, s]
        )

    token_steps = token_width // 256

    def finish(s):
        def after_piece(lo, hi):
            x = stream_rows(s, first + lo, first + hi).astype(F32)
            y = (x + join(gate0_own, gate0, lo, hi) * dot(blend_ref[s, lo:hi], out_w_ref[...])).astype(BF16)
            after_ref[s, lo:hi] = y
            trans_ref[s, lo:hi] = attn_rows(
                y, join(scale1_own, scale1, lo, hi), join(shift1_own, shift1, lo, hi)
            )

        def hidden_piece(lo, hi):
            y = dot(trans_ref[s, lo:hi], swiglu_ref[...])
            a = y[:, :hidden]
            hidden_ref[s, lo:hi] = (a * sigmoid(a) * y[:, hidden:]).astype(BF16)

        def result_piece(lo, hi):
            y = join(gate1_own, gate1, lo, hi) * dot(hidden_ref[s, lo:hi], down_ref[...])
            result_ref[s, lo:hi] = (after_ref[s, lo:hi].astype(F32) + y).astype(BF16)

        def feature_piece(lo, hi):
            y = dot(result_ref[s, lo:hi], token_w_ref[...])
            feature_ref[s % 2, lo:hi] = jnp.maximum(y, 0.0).astype(BF16)

        def token_piece(lo, hi):
            y = dot(onehot_ref[:, :rows], feature_ref[s % 2, :, lo:hi])
            for c in range(lo, hi, 128):
                z = y[:, c - lo : c - lo + 128] * inverse_ref[...]
                tokens_ref[s, :, c : c + 128] = z.astype(BF16)
            token_copy(s, lo // 256).start()

        stages = (after_piece, hidden_piece, result_piece, feature_piece)
        out = skew(*[each(f, rows, PIECES) for f in stages])
        out.append(lambda: atom_copy(s).start())
        out += [lambda lo=lo: token_piece(lo, lo + 256) for lo in range(0, token_width, 256)]
        return out

    weave(lead())
    for s in range(samples):
        weave(
            attend(s),
            finish(s - 1) if s > 0 else None,
            prepare(s + 1) if s + 1 < samples else None,
        )
    weave(finish(samples - 1))
    for s in range(samples):
        atom_copy(s).wait()
        for n in range(token_steps):
            token_copy(s, n).wait()


def on_device(
    atoms_in,
    cond,
    pair,
    atom_mask,
    atom_count,
    atom_to_token,
    ada_weight,
    ada_bias,
    zero_weight,
    zero_bias,
    qkvg_weight,
    query_bias,
    pair_weight,
    out_weight,
    swiglu_weight,
    down_weight,
    token_weight,
):
    samples, atom_dev, width = atoms_in.shape
    windows, query_len, channels, key_len = pair.shape
    count_row = jnp.broadcast_to(atom_count, (8, 128))
    heads = pair_weight.shape[0]
    hidden = down_weight.shape[0]
    token_width = token_weight.shape[1]
    tok_dev = atom_dev // ATOMS_PER_TOKEN
    ext = atom_dev + 2 * HALO
    rows = atom_dev + 2 * EDGE
    far = pl.BlockSpec(memory_space=pltpu.HBM)
    vmem = pl.BlockSpec(memory_space=pltpu.VMEM)

    def near(array):
        return pltpu.with_memory_space_constraint(array, pltpu.VMEM)

    def away(array):
        return pltpu.with_memory_space_constraint(array, pltpu.HBM)

    wire_rows = (samples + 1) * HALO + EDGE_Q * channels + 16
    wire = pltpu.VMEM((wire_rows, width), BF16)
    pair = pair.reshape(windows, query_len * channels, key_len)
    across, within, info = pl.pallas_call(
        pack_kernel,
        out_shape=(wire, wire, pltpu.VMEM((16, atom_dev), F32)),
        in_specs=[far] * 5,
        out_specs=(vmem, vmem, vmem),
        scratch_shapes=[
            pltpu.VMEM((atom_dev,), jnp.int32),
            pltpu.VMEM((atom_dev,), jnp.int32),
            pltpu.SemaphoreType.DMA((2 * (samples + 3),)),
        ],
        compiler_params=pltpu.CompilerParams(vmem_limit_bytes=4 << 20),
        name="pack",
    )(*[away(a) for a in (atom_mask, atom_to_token, atoms_in, cond, pair)])
    count = lax.axis_size("atom")
    swaps = [[(i, i + 1) for i in range(at, count - 1, 2)] for at in (1, 0)]
    swaps = [pairs + [(j, i) for i, j in pairs] for pairs in swaps]
    across = lax.ppermute(across, "atom", swaps[0])
    within = lax.ppermute(within, "atom", swaps[1])

    lhs_shape = (3 * 16 * heads, 16 * channels)
    shared = [
        near(a)
        for a in (
            atoms_in,
            ada_bias,
            zero_bias,
            query_bias.reshape(1, width),
        )
    ]
    near_atoms, ada_b, zero_b, query_b = shared
    early_weights = (ada_weight, zero_weight, qkvg_weight)
    ada_w, zero_w, qkvg_w = [away(a) for a in early_weights]
    near_count = near(count_row)
    own_rows = pltpu.VMEM((atom_dev, width), F32)
    own_half = pltpu.VMEM((atom_dev, width), BF16)
    early = pl.pallas_call(
        early_kernel,
        out_shape=(
            pltpu.VMEM((windows, heads * query_len, key_len), F32),
            pltpu.VMEM(lhs_shape, BF16),
        )
        + (own_rows,) * 6
        + (own_half,) * 3
        + (own_rows, pltpu.VMEM((width, 2 * width), BF16))
        + tuple(pltpu.VMEM(a.shape, a.dtype) for a in early_weights),
        in_specs=[vmem] * 6 + [far, vmem, far, vmem, far, vmem],
        out_specs=(vmem,) * 16,
        scratch_shapes=[
            pltpu.VMEM((4, 16 * heads, key_len), F32),
            pltpu.VMEM((4, 2, 128, key_len), BF16),
            pltpu.VMEM((16, key_len), F32),
            pltpu.VMEM((atom_dev, width), BF16),
            pltpu.VMEM((atom_dev, width), BF16),
            pltpu.SemaphoreType.DMA((3,)),
        ],
        compiler_params=pltpu.CompilerParams(
            vmem_limit_bytes=8 << 20
        ),
        name="early",
    )(
        near_count, near(pair_weight), near(info), near(pair), near(cond), near_atoms,
        ada_w,
        ada_b,
        zero_w,
        zero_b,
        qkvg_w,
        query_b,
    )
    ada_w, zero_w, qkvg_w = [near(a) for a in early[13:]]
    first_weights = (ada_w, ada_b, zero_w, zero_b, qkvg_w, query_b)

    last_weights = [near(a) for a in (out_weight, swiglu_weight, down_weight, token_weight)]
    operands = [near_atoms, near_count] + [near(a) for a in (info, across, within, *early[:13])]
    operands += [*first_weights, *last_weights]
    return pl.pallas_call(
        block_kernel,
        out_shape=(
            jax.ShapeDtypeStruct((samples, atom_dev, width), BF16),
            jax.ShapeDtypeStruct((samples, tok_dev, token_width), BF16),
        ),
        in_specs=[vmem] * len(operands),
        out_specs=(far, far),
        scratch_shapes=[
            pltpu.VMEM((2 * HALO, width), F32),
            pltpu.VMEM((2 * HALO, width), F32),
            pltpu.VMEM((2 * EDGE, width), F32),
            pltpu.VMEM((2 * EDGE, width), F32),
            pltpu.VMEM((2 * EDGE, width), F32),
            pltpu.VMEM((2 * EDGE, width), F32),
            pltpu.VMEM((2, heads * EDGE_Q, key_len), F32),
            pltpu.VMEM((16, key_len), F32),
            pltpu.VMEM((tok_dev, 512), BF16),
            pltpu.VMEM((tok_dev, 128), F32),
            pltpu.VMEM((wire_rows, width), BF16),
            pltpu.VMEM((wire_rows, width), BF16),
            pltpu.VMEM((samples, ext, width), BF16),
            pltpu.VMEM((samples, rows, width), BF16),
            pltpu.VMEM((samples, ext, width), BF16),
            pltpu.VMEM((samples, ext, width), BF16),
            pltpu.VMEM((samples, rows, width), F32),
            pltpu.VMEM((2, windows + 2, heads * query_len, key_len), F32),
            pltpu.VMEM((2, windows + 2, heads * query_len, key_len), BF16),
            pltpu.VMEM((2, windows + 2, query_len, width), F32),
            pltpu.VMEM((samples, rows, width), BF16),
            pltpu.VMEM((samples, rows, width), BF16),
            pltpu.VMEM((samples, rows, width), BF16),
            pltpu.VMEM((samples, rows, hidden), BF16),
            pltpu.VMEM((samples, rows, width), BF16),
            pltpu.VMEM((2, rows, token_width), BF16),
            pltpu.VMEM((samples, tok_dev, token_width), BF16),
            pltpu.SemaphoreType.DMA((1 + token_width // 256, samples)),
        ],
        compiler_params=pltpu.CompilerParams(vmem_limit_bytes=24 << 20),
        name="block",
    )(*operands)


def solution(mesh):
    in_specs = (
        P("struct", "atom", None),
        P(("struct", "atom"), None),
        P(("struct", "atom"), None, None, None),
        P(("struct", "atom")),
        P("struct"),
        P(("struct", "atom")),
        P(),
        P(),
        P(),
        P(),
        P(),
        P(),
        P(),
        P(),
        P(),
        P(),
        P(),
    )
    out_specs = (P("struct", "atom", None), P("struct", "atom", None))
    return jax.shard_map(
        on_device, mesh=mesh, in_specs=in_specs, out_specs=out_specs, check_vma=False
    )
```
